32 devices in a mesh: groups: 2 (over y), tile: 4 (over x, core), slab: 4 (over z).
Axes of the slice: x: 2, y: 2, z: 4, core: 2. Of those that a mesh axis runs over, the one named last changes fastest.
Arguments:
- start_states: float32 [8, 49, 256, 128], P(('groups', 'slab'), None, 'tile'), parts along dimension 0, may hold values from -6 to 6
- end_adjoints: float32 [8, 49, 256, 128], P(('groups', 'slab'), None, 'tile'), parts along dimension 0, may hold values from -6 to 6
- misfits: float32 [8, 4, 256, 128], P(('groups', 'slab'), None, 'tile'), parts along dimension 0, may hold values from -6 to 6
- water_depth: float32 [512, 128], P(('groups', 'tile')), parts along dimension 0, may hold values from 0.5 to 2
- drag_coef: float32 [512, 128], P(('groups', 'tile')), parts along dimension 0, may hold values from 0.5 to 2
- sea_mask: int32 [512, 128], P(('groups', 'tile')), parts along dimension 0, may hold values 0 or 1
- bottom_level: int32 [512, 128], P(('groups', 'tile')), parts along dimension 0, may hold values from 1 to 24
Outputs:
- next_starts: float32 [8, 49, 256, 128], P(('groups', 'slab'), None, 'tile'), parts along dimension 0
- next_end_adjoints: float32 [8, 49, 256, 128], P(('groups', 'slab'), None, 'tile'), parts along dimension 0
- drag_gradient: float32 [512, 128], P(('groups', 'tile')), parts along dimension 0
The draws below stay inside these ranges and needn't reach their ends.
There are 2 independent parts, one for each index of `groups`. The reference program is written for one: setup_inputs(seed, part) draws one part's arguments, and reference() takes and returns one part's arrays. A program takes and returns all parts, laid end to end along the dimension named above; each array names one. Nothing has to cross between parts.
Inputs may be any that keep to these rules, and one draw needn't show every extreme that they name: `sea_mask`: 1 for a sea column, 0 for a land column.
All inputs are finite; a program needn't handle non-finite values. No bound on the sum of `sea_mask` on one device may be relied on, other than what follows from the above.
Results may differ from the reference program's by a relative error of at most 0.0003.
Values sent between devices are 32-bit elements; how exact they have to be, the bound alone decides.
No kernel may reach another device: no remote copies, remote signals or barrier semaphores. Data moves between devices by JAX's collectives and lax.ppermute only.
A program may use at most 64 MiB of HBM per device.

```python
import math
import jax
import jax.numpy as jnp
from jax import lax

LEVELS = 24
STEPS = 4
NY = 128
FIELDS = 49
NX = 256
SLABS = 4


def touch_ends(values, rng, least, high):
    longest = values.shape.index(max(values.shape))
    spots = []
    for shift in (0, 1):
        where = [jax.random.randint(jax.random.fold_in(rng, axis), (), 0, length) for axis, length in enumerate(values.shape)]
        where[longest] = (where[longest] + shift) % values.shape[longest]
        spots.append(tuple(where))
    return values.at[spots[0]].set(least).at[spots[1]].set(high)


def shard_levels(key, shape, split, low, high):
    def one(position, parts):
        heights = jax.random.uniform(jax.random.fold_in(jax.random.fold_in(key, 6), position), (parts,), jnp.float32, low / len(split), high / len(split))
        return jnp.repeat(jnp.exp(heights), shape[position] // parts).reshape((-1,) + (1,) * (len(shape) - position - 1))

    loudness = one(*split[0])
    for cut in split[1:]:
        loudness = loudness * one(*cut)
    return loudness


def gaussian(own_key, dims, deviation, reach, split=(), dtype=jnp.bfloat16):
    values = deviation * jax.random.normal(own_key, dims, jnp.float32)
    if split:
        values = values * shard_levels(own_key, dims, split, -0.22, 0.18)
    return jnp.clip(values, -reach, reach).astype(dtype)


def setup_inputs(seed: int = 0, part: int = 0) -> dict:
    keys = jax.random.split(jax.random.key(seed), 8)
    own_keys = jax.random.split(jax.random.fold_in(keys[7], part), 8)
    start_states = gaussian(own_keys[0], (SLABS, FIELDS, NX, NY), 1.0, 6.0, ((0, 4), (2, 4)), jnp.float32)
    end_adjoints = gaussian(own_keys[1], (SLABS, FIELDS, NX, NY), 1.0, 6.0, ((0, 4), (2, 4)), jnp.float32)
    misfits = gaussian(own_keys[2], (SLABS, STEPS, NX, NY), 1.0, 6.0, ((0, 4), (2, 4)), jnp.float32)
    water_depth = jnp.clip(jnp.exp(math.log(2.0) - 1.3862944 * jax.random.uniform(own_keys[3], (NX, NY), jnp.float32) ** shard_levels(own_keys[3], (NX, NY), ((0, 4),), -0.2, 0.2)), 0.5, 2.0)
    drag_coef = jnp.clip(jnp.exp(math.log(2.0) - 1.3862944 * jax.random.uniform(own_keys[4], (NX, NY), jnp.float32) ** shard_levels(own_keys[4], (NX, NY), ((0, 4),), -0.2, 0.2)), 0.5, 2.0)
    sea_mask = touch_ends((jax.random.randint(own_keys[5], (NX, NY), 0, 10) < 9).astype(jnp.int32), jax.random.fold_in(own_keys[5], 1), 0, 1)
    bottom_level = touch_ends(jax.random.randint(own_keys[6], (NX, NY), 1, LEVELS + 1), jax.random.fold_in(own_keys[6], 1), 1, LEVELS).astype(jnp.int32)
    return dict(start_states=start_states, end_adjoints=end_adjoints, misfits=misfits, water_depth=water_depth, drag_coef=drag_coef, sea_mask=sea_mask, bottom_level=bottom_level)


def column_diff(values):
    padded = jnp.pad(values, [(0, 0)] * (values.ndim - 1) + [(1, 1)])
    return padded[..., 2:] - padded[..., :-2]

def vertical_mix(values, active_in):
    zeros_row = jnp.zeros_like(values[:1])
    zeros_mask = jnp.zeros_like(active_in[:1])
    upper_level = jnp.concatenate([zeros_row, values[:-1]], 0)
    lower_level = jnp.concatenate([values[1:], zeros_row], 0)
    upper_active = jnp.concatenate([zeros_mask, active_in[:-1]], 0)
    lower_active = jnp.concatenate([active_in[1:], zeros_mask], 0)
    return upper_active * (upper_level - values) + lower_active * (lower_level - values)

def advance(state, statics):
    levels = (state.shape[0] - 1) // 2
    water_depth = statics[0]
    wet_levels = statics[1]
    drag_field = statics[2]
    sea_cells = jnp.minimum(wet_levels, 1.0)
    level_index = jnp.arange(levels).astype(jnp.float32)[:, None, None]
    active = (level_index < wet_levels[None]).astype(jnp.float32)
    bottom = (level_index == wet_levels[None] - 1.0).astype(jnp.float32)
    thickness = water_depth / jnp.maximum(wet_levels, 1.0)
    u_active = state[1:levels + 1] * active
    v_active = state[levels + 1:] * active
    flux_x = thickness * lax.optimization_barrier(jnp.sum(u_active, 0))
    flux_y = thickness * lax.optimization_barrier(jnp.sum(v_active, 0))
    diverge = flux_x[2:] - flux_x[:-2] + column_diff(flux_y)[1:-1]
    surface = sea_cells[1:-1] * (state[0, 1:-1] - 0.2 * diverge)
    slope_x = surface[2:] - surface[:-2]
    slope_y = column_diff(surface)[1:-1]
    u_inner = u_active[:, 2:-2]
    v_inner = v_active[:, 2:-2]
    active_in = active[:, 2:-2]
    bottom_in = bottom[:, 2:-2]
    thick_in = thickness[2:-2]
    sea_in = sea_cells[2:-2]
    drag_in = drag_field[2:-2]
    u_next = u_inner + 0.1 * v_inner - 0.2 * slope_x + 0.1 * vertical_mix(u_inner, active_in)
    v_next = v_inner - 0.1 * u_inner - 0.2 * slope_y + 0.1 * vertical_mix(v_inner, active_in)
    u_bottom = lax.optimization_barrier(jnp.sum(bottom_in * u_inner, 0))
    v_bottom = lax.optimization_barrier(jnp.sum(bottom_in * v_inner, 0))
    bottom_speed = jnp.sqrt(u_bottom * u_bottom + v_bottom * v_bottom + 0.0025)
    factor = thick_in / (thick_in + 0.1 * drag_in * bottom_speed + 1.0 - sea_in)
    retain = sea_in * active_in * (1.0 - bottom_in + bottom_in * factor)
    return jnp.concatenate([surface[1:-1][None], u_next * retain, v_next * retain], 0)

def reference(start_states, end_adjoints, misfits, water_depth, drag_coef, sea_mask, bottom_level):
    wet_levels = (sea_mask * bottom_level).astype(jnp.float32)

    def one_slab(inputs):
        initial, adjoint, misfit_slab = inputs

        def march_all(state, drag_field):
            statics = jnp.stack([water_depth, wet_levels, drag_field])
            stat_pad = jnp.pad(statics, ((0, 0), (2, 2), (0, 0)))
            surfaces = []
            for number in range(STEPS):
                state = advance(jnp.pad(state, ((0, 0), (2, 2), (0, 0))), stat_pad)
                surfaces.append(state[0])
            return (jnp.stack(surfaces), state)
        (surfaces, final_state), pullback = jax.vjp(march_all, initial, drag_coef)
        start_adjoint, drag_grads = pullback((misfit_slab, adjoint))
        return (final_state, start_adjoint, drag_grads)
    final_states, start_adjoints, drag_grads = lax.map(one_slab, (start_states, end_adjoints, misfits))
    return (jnp.roll(final_states, 1, 0), jnp.roll(start_adjoints, -1, 0), lax.optimization_barrier(jnp.sum(drag_grads, 0)))
```

```python
import jax
import jax.numpy as jnp
from jax import lax
from jax.experimental import pallas as pl
from jax.experimental.pallas import tpu as pltpu
from jax.sharding import PartitionSpec as P

STEPS = 4
BLOCK = 8
HALO = 2 * STEPS
SAVED = 2 + 2 * STEPS


def shifted(block, axis, distance):
    devices = range(lax.axis_size(axis))
    route = [(i - distance, i) for i in devices if i - distance in devices]
    return lax.ppermute(block, axis, route)


def passed_along(block, axis, distance):
    devices = range(lax.axis_size(axis))
    route = [((i - distance) % len(devices), i) for i in devices]
    return lax.ppermute(block, axis, route)


def row_diff(values):
    return pltpu.roll(values, values.shape[0] - 1, 0) - pltpu.roll(values, 1, 0)


def column_diff(values):
    width = values.shape[1]
    lane = lax.broadcasted_iota(jnp.int32, values.shape, 1)
    after = jnp.where(lane < width - 1, pltpu.roll(values, width - 1, 1), 0.0)
    before = jnp.where(lane > 0, pltpu.roll(values, 1, 1), 0.0)
    return after - before


def over_blocks(rows, with_halo, visit, own, above, below):
    if with_halo:
        visit(pl.ds(0, BLOCK), above, pl.ds(0, BLOCK))

    def inner(index, carry):
        start = pl.multiple_of(index * BLOCK, BLOCK)
        visit(pl.ds(pl.multiple_of(start + HALO, BLOCK), BLOCK), own, pl.ds(start, BLOCK))
        return carry

    lax.fori_loop(0, rows // BLOCK, inner, 0)
    if with_halo:
        visit(pl.ds(HALO + rows, BLOCK), below, pl.ds(0, BLOCK))


def fill_padded(target, own, above, below):
    rows = own.shape[0]
    target[0:HALO] = above
    target[HALO : HALO + rows] = own
    target[HALO + rows : rows + 2 * HALO] = below


def drag_terms(u_bottom, v_bottom, thickness, drag, sea):
    speed = jnp.sqrt(u_bottom * u_bottom + v_bottom * v_bottom + 0.0025)
    denominator = thickness + 0.1 * drag * speed + 1.0 - sea
    return speed, denominator, thickness / denominator


def forward_kernel(state, above, below, depth, wet, drag, final, saved,
                   work, wet_pad, thick, drag_pad, eta, sum_u, sum_v, bot_u, bot_v, slope_x, slope_y, factor):
    fields, rows, _ = state.shape
    levels = (fields - 1) // 2
    fill_padded(wet_pad, wet[...], above[fields + 1], below[fields + 1])
    fill_padded(drag_pad, drag[...], above[fields + 2], below[fields + 2])
    fill_padded(thick, depth[...], above[fields], below[fields])
    fill_padded(eta, state[0], above[0], below[0])
    thick[...] = thick[...] / jnp.maximum(wet_pad[...], 1.0)

    def sums(at, source, source_at):
        wet_here = wet_pad[at]
        total_u = total_v = low_u = low_v = jnp.zeros_like(wet_here)
        for level in range(levels):
            active = wet_here > level
            bottom = wet_here == level + 1
            u = jnp.where(active, source[1 + level, source_at], 0.0)
            v = jnp.where(active, source[1 + levels + level, source_at], 0.0)
            total_u += u
            total_v += v
            low_u = jnp.where(bottom, u, low_u)
            low_v = jnp.where(bottom, v, low_v)
        sum_u[at] = total_u
        sum_v[at] = total_v
        bot_u[at] = low_u
        bot_v[at] = low_v

    over_blocks(rows, True, sums, state, above, below)
    saved[0] = bot_u[HALO : HALO + rows]
    saved[1] = bot_v[HALO : HALO + rows]

    for step in range(STEPS):
        first, last = step == 0, step == STEPS - 1
        sea = jnp.minimum(wet_pad[...], 1.0)
        flux_x = thick[...] * sum_u[...]
        flux_y = thick[...] * sum_v[...]
        surface = sea * (eta[...] - 0.2 * (row_diff(flux_x) + column_diff(flux_y)))
        eta[...] = surface
        slope_x[...] = 0.2 * row_diff(surface)
        slope_y[...] = 0.2 * column_diff(surface)
        factor[...] = drag_terms(bot_u[...], bot_v[...], thick[...], drag_pad[...], sea)[2]

        def update(at, source, source_at):
            wet_here = wet_pad[at]
            slow = factor[at]
            grad_x = slope_x[at]
            grad_y = slope_y[at]
            zero = jnp.zeros_like(wet_here)
            total_u = total_v = low_u = low_v = zero

            def fetch(level):
                if level == levels:
                    return zero, zero
                u = source[1 + level, source_at]
                v = source[1 + levels + level, source_at]
                if first:
                    u = jnp.where(wet_here > level, u, 0.0)
                    v = jnp.where(wet_here > level, v, 0.0)
                return u, v

            u_up = v_up = zero
            u, v = fetch(0)
            for level in range(levels):
                u_down, v_down = fetch(level + 1)
                inside = wet_here > level + 1
                bottom = wet_here == level + 1
                own = 1.0 if level == 0 else 0.9
                weight = jnp.where(inside, own - 0.1, own)
                retain = jnp.where(inside, 1.0, jnp.where(bottom, slow, 0.0))
                ut = weight * u + 0.1 * (v + u_up + u_down) - grad_x
                vt = weight * v + 0.1 * (v_up + v_down - u) - grad_y
                low_u = jnp.where(bottom, ut, low_u)
                low_v = jnp.where(bottom, vt, low_v)
                u_new = ut * retain
                v_new = vt * retain
                if last:
                    final[1 + level, source_at] = u_new
                    final[1 + levels + level, source_at] = v_new
                else:
                    work[1 + level, at] = u_new
                    work[1 + levels + level, at] = v_new
                    total_u += u_new
                    total_v += v_new
                u_up, v_up, u, v = u, v, u_down, v_down
            sum_u[at] = total_u
            sum_v[at] = total_v
            bot_u[at] = low_u
            bot_v[at] = low_v

        if first:
            over_blocks(rows, True, update, state, above, below)
        else:
            def inner(index, carry):
                start = pl.multiple_of(index * BLOCK, BLOCK)
                if last:
                    at = pl.ds(pl.multiple_of(start + HALO, BLOCK), BLOCK)
                    load = at
                else:
                    at = load = pl.ds(start, BLOCK)

                class Source:
                    def __getitem__(self, key):
                        return work[key[0], load]

                update(at, Source(), pl.ds(start, BLOCK))
                return carry

            lax.fori_loop(0, rows // BLOCK if last else (rows + 2 * HALO) // BLOCK, inner, 0)
        saved[2 + 2 * step] = bot_u[HALO : HALO + rows]
        saved[3 + 2 * step] = bot_v[HALO : HALO + rows]
        bot_u[...] = factor[...] * bot_u[...]
        bot_v[...] = factor[...] * bot_v[...]
    final[0] = eta[HALO : HALO + rows]


def adjoint_kernel(adjoint, misfit, saved, above, below, depth, wet, drag, stat_above, stat_below,
                   start, gradient,
                   work, kept, wet_pad, thick, drag_pad, eta, sum_u, sum_v, bot_u, bot_v,
                   push_x, push_y, push_low_x, push_low_y, factor, grad_pad):
    fields, rows, _ = adjoint.shape
    levels = (fields - 1) // 2
    miss_at, saved_at = fields, fields + STEPS
    fill_padded(wet_pad, wet[...], stat_above[1], stat_below[1])
    fill_padded(drag_pad, drag[...], stat_above[2], stat_below[2])
    fill_padded(thick, depth[...], stat_above[0], stat_below[0])
    thick[...] = thick[...] / jnp.maximum(wet_pad[...], 1.0)
    for item in range(SAVED):
        fill_padded(kept.at[item], saved[item], above[saved_at + item], below[saved_at + item])
    fill_padded(eta, adjoint[0], above[0], below[0])
    grad_pad[...] = jnp.zeros_like(grad_pad)
    sea = jnp.minimum(wet_pad[...], 1.0)

    before = [(kept[0], kept[1])]
    for step in range(STEPS - 1):
        slow = drag_terms(*before[step], thick[...], drag_pad[...], sea)[2]
        before.append((slow * kept[2 + 2 * step], slow * kept[3 + 2 * step]))

    def sums(at, source, source_at):
        wet_here = wet_pad[at]
        total_u = total_v = low_u = low_v = jnp.zeros_like(wet_here)
        for level in range(levels):
            active = wet_here > level
            bottom = wet_here == level + 1
            u = jnp.where(active, source[1 + level, source_at], 0.0)
            v = jnp.where(active, source[1 + levels + level, source_at], 0.0)
            total_u += u
            total_v += v
            low_u = jnp.where(bottom, u, low_u)
            low_v = jnp.where(bottom, v, low_v)
        sum_u[at] = total_u
        sum_v[at] = total_v
        bot_u[at] = low_u
        bot_v[at] = low_v

    over_blocks(rows, True, sums, adjoint, above, below)

    for step in reversed(range(STEPS)):
        first, last = step == STEPS - 1, step == 0
        sea = jnp.minimum(wet_pad[...], 1.0)
        fill_padded(push_x, misfit[step], above[miss_at + step], below[miss_at + step])
        u_before, v_before = before[step]
        speed, denominator, slow = drag_terms(u_before, v_before, thick[...], drag_pad[...], sea)
        factor[...] = slow
        low_u, low_v = bot_u[...], bot_v[...]
        on_factor = low_u * kept[2 + 2 * step] + low_v * kept[3 + 2 * step]
        on_denominator = -on_factor * slow / denominator
        grad_pad[...] += 0.1 * speed * on_denominator
        on_speed = 0.1 * drag_pad[...] * on_denominator / speed
        loss = 1.0 - slow
        total_x = sum_u[...] - loss * low_u
        total_y = sum_v[...] - loss * low_v
        surface = sea * (eta[...] + push_x[...] + 0.2 * (row_diff(total_x) + column_diff(total_y)))
        eta[...] = surface
        thin = 0.2 * thick[...]
        toward_x = thin * row_diff(surface)
        toward_y = thin * column_diff(surface)
        push_x[...] = toward_x
        push_y[...] = toward_y
        push_low_x[...] = toward_x + on_speed * u_before
        push_low_y[...] = toward_y + on_speed * v_before

        def update(at, source, source_at):
            wet_here = wet_pad[at]
            slow_here = factor[at]
            along_x, along_y = push_x[at], push_y[at]
            low_x, low_y = push_low_x[at], push_low_y[at]
            zero = jnp.zeros_like(wet_here)
            total_u = total_v = low_u = low_v = zero

            def fetch(level):
                if level == levels:
                    return zero, zero
                retain = jnp.where(wet_here > level + 1, 1.0, jnp.where(wet_here > level, slow_here, 0.0))
                return retain * source[1 + level, source_at], retain * source[1 + levels + level, source_at]

            p_up = q_up = zero
            p, q = fetch(0)
            for level in range(levels):
                p_down, q_down = fetch(level + 1)
                inside = wet_here > level + 1
                bottom = wet_here == level + 1
                active = wet_here > level
                own = 1.0 if level == 0 else 0.9
                weight = jnp.where(inside, own - 0.1, own)
                u = weight * p + 0.1 * (p_up + p_down - q) + jnp.where(inside, along_x, low_x)
                v = weight * q + 0.1 * (q_up + q_down + p) + jnp.where(inside, along_y, low_y)
                u = jnp.where(active, u, 0.0)
                v = jnp.where(active, v, 0.0)
                if last:
                    start[1 + level, source_at] = u
                    start[1 + levels + level, source_at] = v
                else:
                    work[1 + level, at] = u
                    work[1 + levels + level, at] = v
                    total_u += u
                    total_v += v
                    low_u = jnp.where(bottom, u, low_u)
                    low_v = jnp.where(bottom, v, low_v)
                p_up, q_up, p, q = p, q, p_down, q_down
            if not last:
                sum_u[at] = total_u
                sum_v[at] = total_v
                bot_u[at] = low_u
                bot_v[at] = low_v

        if first:
            over_blocks(rows, True, update, adjoint, above, below)
        else:
            def inner(index, carry):
                begin = pl.multiple_of(index * BLOCK, BLOCK)
                if last:
                    at = pl.ds(pl.multiple_of(begin + HALO, BLOCK), BLOCK)
                    load = at
                else:
                    at = load = pl.ds(begin, BLOCK)

                class Source:
                    def __getitem__(self, key):
                        return work[key[0], load]

                update(at, Source(), pl.ds(begin, BLOCK))
                return carry

            lax.fori_loop(0, rows // BLOCK if last else (rows + 2 * HALO) // BLOCK, inner, 0)
    start[0] = eta[HALO : HALO + rows]
    gradient[...] = grad_pad[HALO : HALO + rows]


def body(start_states, end_adjoints, misfits, water_depth, drag_coef, sea_mask, bottom_level):
    initial = start_states[0]
    adjoint = end_adjoints[0]
    misfit = misfits[0]
    fields, rows, width = initial.shape
    wet = (sea_mask * bottom_level).astype(jnp.float32)
    statics = jnp.stack([water_depth, wet, drag_coef])
    pad = pltpu.VMEM((rows + 2 * HALO, width), jnp.float32)
    work = pltpu.VMEM((fields, rows + 2 * HALO, width), jnp.float32)
    params = pltpu.CompilerParams(vmem_limit_bytes=32 << 20)
    cells = fields * rows * width

    above = shifted(jnp.concatenate([initial[:, -HALO:], statics[:, -HALO:]]), "tile", 1)
    below = shifted(jnp.concatenate([initial[:, :HALO], statics[:, :HALO]]), "tile", -1)
    final, saved = pl.pallas_call(
        forward_kernel,
        out_shape=(
            jax.ShapeDtypeStruct((fields, rows, width), jnp.float32),
            jax.ShapeDtypeStruct((SAVED, rows, width), jnp.float32),
        ),
        scratch_shapes=[work] + [pad] * 11,
        compiler_params=params,
        cost_estimate=pl.CostEstimate(flops=100 * cells, bytes_accessed=10 * cells, transcendentals=0),
        name="forward",
    )(initial, above, below, water_depth, wet, drag_coef)
    next_state = passed_along(final, "slab", 1)

    low = jnp.concatenate([adjoint[:, -HALO:], misfit[:, -HALO:], saved[:, -HALO:]])
    high = jnp.concatenate([adjoint[:, :HALO], misfit[:, :HALO], saved[:, :HALO]])
    start, gradient = pl.pallas_call(
        adjoint_kernel,
        out_shape=(
            jax.ShapeDtypeStruct((fields, rows, width), jnp.float32),
            jax.ShapeDtypeStruct((rows, width), jnp.float32),
        ),
        scratch_shapes=[work, pltpu.VMEM((SAVED, rows + 2 * HALO, width), jnp.float32)] + [pad] * 14,
        compiler_params=params,
        cost_estimate=pl.CostEstimate(flops=100 * cells, bytes_accessed=10 * cells, transcendentals=0),
        name="adjoint",
    )(adjoint, misfit, saved, shifted(low, "tile", 1), shifted(high, "tile", -1),
      water_depth, wet, drag_coef, above[fields:], below[fields:])
    next_adjoint = passed_along(start, "slab", -1)
    drag_total = lax.psum(gradient, "slab")
    return (next_state[None], next_adjoint[None], drag_total)


def solution(mesh):
    return jax.shard_map(
        body,
        mesh=mesh,
        in_specs=(
            P(("groups", "slab"), None, "tile", None),
            P(("groups", "slab"), None, "tile", None),
            P(("groups", "slab"), None, "tile", None),
            P(("groups", "tile"), None),
            P(("groups", "tile"), None),
            P(("groups", "tile"), None),
            P(("groups", "tile"), None),
        ),
        out_specs=(
            P(("groups", "slab"), None, "tile", None),
            P(("groups", "slab"), None, "tile", None),
            P(("groups", "tile"), None),
        ),
        check_vma=False,
    )
```

```python
import jax
import jax.numpy as jnp
from jax import lax
from jax.experimental import pallas as pl
from jax.experimental.pallas import tpu as pltpu
from jax.sharding import PartitionSpec as P

STEPS = 4
BLOCK = 8
HALO = 2 * STEPS
REACH = 2 * HALO
SAVED = 2 + 2 * STEPS
POOL = 4 * BLOCK
SLOTS = 29


def shifted(block, axis, distance):
    devices = range(lax.axis_size(axis))
    route = [(i - distance, i) for i in devices if i - distance in devices]
    return lax.ppermute(block, axis, route)


def passed_along(block, axis, distance):
    devices = range(lax.axis_size(axis))
    route = [((i - distance) % len(devices), i) for i in devices]
    return lax.ppermute(block, axis, route)


def row_diff(values):
    return pltpu.roll(values, values.shape[0] - 1, 0) - pltpu.roll(values, 1, 0)


def column_diff(values):
    width = values.shape[1]
    lane = lax.broadcasted_iota(jnp.int32, values.shape, 1)
    after = jnp.where(lane < width - 1, pltpu.roll(values, width - 1, 1), 0.0)
    before = jnp.where(lane > 0, pltpu.roll(values, 1, 1), 0.0)
    return after - before


def looped(count, visit):
    def one(index, carry):
        visit(pl.multiple_of(index * BLOCK, BLOCK))
        return carry

    lax.fori_loop(0, count // BLOCK, one, 0)


def over_blocks(rows, halo, visit, own, above, below):
    block = lambda start: pl.ds(start if isinstance(start, int) else pl.multiple_of(start, BLOCK), BLOCK)
    looped(halo, lambda start: visit(block(start), above, block(start)))
    looped(rows, lambda start: visit(block(start + halo), own, block(start)))
    looped(halo, lambda start: visit(block(start + halo + rows), below, block(start)))


def fill_padded(target, own, above, below):
    rows, halo = own.shape[0], above.shape[0]
    target[0:halo] = above
    target[halo : halo + rows] = own
    target[halo + rows : rows + 2 * halo] = below


class Shifted:
    def __init__(self, ref, at):
        self.ref, self.at = ref, at

    def __getitem__(self, key):
        return self.ref[key[0], self.at]


class AdjointEdge:
    def __init__(self, ref, fields):
        self.ref, self.fields = ref, fields

    def __getitem__(self, key):
        plane, rows = edge_place(self.fields, key[0])
        return self.ref[plane, rows]


def edge_planes(fields):
    return fields + 3 + (fields + STEPS + 1) // 2


def edge_place(fields, item):
    first = (fields + STEPS + 1) // 2
    half = 0 if item < first else HALO
    return fields + 3 + item - (first if half else 0), pl.ds(half, HALO)


def lanes_of(values):
    return lax.broadcasted_iota(jnp.int32, values.shape, values.ndim - 1)


def take_lanes(values, index):
    return jnp.take_along_axis(values, index, axis=1, mode="promise_in_bounds")


def plan_kernel(mask, bottom, wet, order, place, deepest):
    rows, width = mask.shape
    half = width // 2
    depth = mask[...] * bottom[...]
    wet[...] = depth.astype(jnp.float32)
    lane = lanes_of(depth)
    even = (lax.broadcasted_iota(jnp.int32, depth.shape, 0) // BLOCK) % 2 == 0
    key = (depth * width + lane).astype(jnp.float32)
    rank = jnp.zeros_like(depth)
    for shift in range(1, width):
        rank = rank + jnp.where(pltpu.roll(key, shift, 1) > key, 1, 0)
    ahead = jnp.where(rank < half, rank, width + half - 1 - rank)
    behind = jnp.where(rank < half, rank + half, width - 1 - rank)
    there = jnp.where(even, ahead, behind)
    place[...] = there
    moved = jnp.zeros_like(depth)
    for shift in range(1, width):
        moved = jnp.where(pltpu.roll(there, shift, 1) == lane, shift, moved)
    origin = (lane - moved) & (width - 1)
    order[...] = origin
    most = jnp.zeros((BLOCK, width), jnp.float32)
    for pool in range(rows // POOL):
        ats = [slice(pool * POOL + block * BLOCK, pool * POOL + (block + 1) * BLOCK) for block in range(4)]
        deep, shallow, swap = pair_up([take_lanes(wet[at], origin[at]) for at in ats])
        most = jnp.maximum(most, deep[0] + jnp.where(swap, shallow[1], shallow[0]))
        most = jnp.maximum(most, deep[1] + jnp.where(swap, shallow[0], shallow[1]))
    deepest[0, 0] = jnp.max(most).astype(jnp.int32)


def deep_and_shallow(blocks):
    first = lanes_of(blocks[0]) < blocks[0].shape[1] // 2
    deep = [jnp.where(first, blocks[0], blocks[1]), jnp.where(first, blocks[2], blocks[3])]
    shallow = [jnp.where(first, blocks[1], blocks[0]), jnp.where(first, blocks[3], blocks[2])]
    return deep, shallow


def pair_up(depths):
    deep, shallow = deep_and_shallow(depths)
    swap = (deep[0] - deep[1]) * (shallow[0] - shallow[1]) > 0.0
    return deep, shallow, swap


def pool_rows(pool):
    start = pl.multiple_of(pool * POOL, POOL)
    return [pl.ds(pl.multiple_of(start + block * BLOCK, BLOCK), BLOCK) for block in range(4)]


def pool_slots(pool):
    start = pl.multiple_of(pool * (POOL // 2), POOL // 2)
    return [pl.ds(pl.multiple_of(start + block * BLOCK, BLOCK), BLOCK) for block in range(2)]


def pack(state, wet, order, packed):
    fields, rows, _ = state.shape
    levels = (fields - 1) // 2

    def one_pool(pool, carry):
        ats = pool_rows(pool)
        slots = pool_slots(pool)
        orders = [order[at, :] for at in ats]
        deep_wet, _, swap = pair_up([take_lanes(wet[at, :], by) for at, by in zip(ats, orders)])
        for base, target in ((1, 0), (1 + levels, SLOTS)):

            def sorted_level(level):
                parts = [take_lanes(state[base + level, at, :], by) for at, by in zip(ats, orders)]
                deep, shallow = deep_and_shallow(parts)
                return deep, (jnp.where(swap, shallow[1], shallow[0]), jnp.where(swap, shallow[0], shallow[1]))

            for near in range((SLOTS + 1) // 2):
                far = SLOTS - 1 - near
                both = far < levels
                deep, shallow = sorted_level(near)
                far_deep, far_shallow = sorted_level(far) if both and far > near else (deep, shallow)
                for half in range(2):
                    value = deep[half]
                    if both:
                        value = jnp.where(deep_wet[half] > near, value, far_shallow[half])
                    packed[target + near, slots[half], :] = value
                    if far > near:
                        value = shallow[half]
                        if both:
                            value = jnp.where(deep_wet[half] > far, far_deep[half], value)
                        packed[target + far, slots[half], :] = value
        for half in range(2):
            for block in range(2):
                packed[2 * SLOTS + half, slots[block], :] = state[0, ats[2 * half + block], :]
        return carry

    lax.fori_loop(0, rows // POOL, one_pool, 0)


def pack_kernel(state, wet, order, packed):
    pack(state, wet, order, packed)


def unpack_kernel(deepest, packed, wet, order, place, whole, state):
    levels = (state.shape[0] - 1) // 2
    pool = pl.program_id(0)

    @pl.when(deepest[0, 0] > SLOTS)
    def _():
        pltpu.sync_copy(whole.at[:, pl.ds(pl.multiple_of(pool * POOL, POOL), POOL), :], state)

    @pl.when(deepest[0, 0] <= SLOTS)
    def _():
        ats = pool_rows(0)
        slots = pool_slots(0)
        wets = [wet[at, :] for at in ats]
        places = [place[at, :] for at in ats]
        _, _, swap = pair_up([take_lanes(depth, order[at, :]) for depth, at in zip(wets, ats)])
        first = lanes_of(swap) < swap.shape[1] // 2
        for base, source in ((1, 0), (1 + levels, SLOTS)):

            def write_level(level, deep, ends):
                shallow = jnp.where(swap, ends[1], ends[0]), jnp.where(swap, ends[0], ends[1])
                for block in range(4):
                    pair = deep[block // 2], shallow[block // 2]
                    if block % 2:
                        pair = pair[::-1]
                    value = take_lanes(jnp.where(first, *pair), places[block])
                    state[base + level, ats[block], :] = jnp.where(wets[block] > level, value, 0.0)

            for near in range((SLOTS + 1) // 2):
                far = SLOTS - 1 - near
                head = [packed[source + near, slot, :] for slot in slots]
                tail = [packed[source + far, slot, :] for slot in slots]
                write_level(near, head, tail)
                if near < far < levels:
                    write_level(far, tail, head)
        for half in range(2):
            for block in range(2):
                state[0, ats[2 * half + block], :] = packed[2 * SLOTS + half, slots[block], :]


def edge_kernel(state, adjoint, misfit, depth, drag, mask, bottom, upward, downward, sems):
    fields, rows, _ = state.shape
    first = (fields + STEPS + 1) // 2
    copies = []
    for side, target in enumerate((upward, downward)):
        wide = pl.ds(side * (rows - REACH), REACH)
        narrow = pl.ds(side * (rows - HALO), HALO)
        joint = fields + 3
        copies += [
            pltpu.make_async_copy(state.at[:, wide, :], target.at[pl.ds(0, fields)], sems.at[3 * side]),
            pltpu.make_async_copy(
                adjoint.at[pl.ds(0, first), narrow, :],
                target.at[pl.ds(joint, first), pl.ds(0, HALO), :],
                sems.at[3 * side + 1],
            ),
            pltpu.make_async_copy(
                adjoint.at[pl.ds(first, fields - first), narrow, :],
                target.at[pl.ds(joint, fields - first), pl.ds(HALO, HALO), :],
                sems.at[3 * side + 2],
            ),
        ]
    for copy in copies:
        copy.start()
    for side, target in enumerate((upward, downward)):
        wide = pl.ds(side * (rows - REACH), REACH)
        narrow = pl.ds(side * (rows - HALO), HALO)
        target[fields] = depth[wide]
        target[fields + 1] = (mask[wide] * bottom[wide]).astype(jnp.float32)
        target[fields + 2] = drag[wide]
        for step in range(STEPS):
            plane, at = edge_place(fields, fields + step)
            target[plane, at] = misfit[step, narrow]
    for copy in copies:
        copy.wait()


def unpack_adjoint_kernel(deepest, packed, wet, order, place, whole, *rest):
    *gradients, state, total = rest
    unpack_kernel(deepest, packed, wet, order, place, whole, state)
    summed = gradients[0][...]
    for gradient in gradients[1:]:
        summed = summed + gradient[...]
    total[...] = summed


def nothing_kernel(result):
    pass


def drag_terms(u_bottom, v_bottom, thickness, drag, sea):
    speed = jnp.sqrt(u_bottom * u_bottom + v_bottom * v_bottom + 0.0025)
    denominator = thickness + 0.1 * drag * speed + 1.0 - sea
    return speed, denominator, thickness / denominator


def forward_kernel(state, above, below, depth, wet, drag, order, final, saved, packed,
                   work, wet_pad, thick, drag_pad, eta, sum_u, sum_v, bot_u, bot_v, slope_x, slope_y, factor):
    fields, rows, _ = state.shape
    levels = (fields - 1) // 2
    fill_padded(wet_pad, wet[...], above[fields + 1], below[fields + 1])
    fill_padded(drag_pad, drag[...], above[fields + 2], below[fields + 2])
    fill_padded(thick, depth[...], above[fields], below[fields])
    fill_padded(eta, state[0], above[0], below[0])
    thick[...] = thick[...] / jnp.maximum(wet_pad[...], 1.0)

    def sums(at, source, source_at):
        wet_here = wet_pad[at]
        total_u = total_v = low_u = low_v = jnp.zeros_like(wet_here)
        for level in range(levels):
            active = wet_here > level
            bottom = wet_here == level + 1
            u = jnp.where(active, source[1 + level, source_at], 0.0)
            v = jnp.where(active, source[1 + levels + level, source_at], 0.0)
            total_u += u
            total_v += v
            low_u = jnp.where(bottom, u, low_u)
            low_v = jnp.where(bottom, v, low_v)
        sum_u[at] = total_u
        sum_v[at] = total_v
        bot_u[at] = low_u
        bot_v[at] = low_v

    over_blocks(rows, REACH, sums, state, above, below)
    saved[0] = bot_u[HALO : REACH + HALO + rows]
    saved[1] = bot_v[HALO : REACH + HALO + rows]

    for step in range(STEPS):
        first, last = step == 0, step == STEPS - 1
        sea = jnp.minimum(wet_pad[...], 1.0)
        flux_x = thick[...] * sum_u[...]
        flux_y = thick[...] * sum_v[...]
        surface = sea * (eta[...] - 0.2 * (row_diff(flux_x) + column_diff(flux_y)))
        eta[...] = surface
        slope_x[...] = 0.2 * row_diff(surface)
        slope_y[...] = 0.2 * column_diff(surface)
        factor[...] = drag_terms(bot_u[...], bot_v[...], thick[...], drag_pad[...], sea)[2]

        def update(at, source, source_at, into_final=False):
            wet_here = wet_pad[at]
            slow = factor[at]
            grad_x = slope_x[at]
            grad_y = slope_y[at]
            zero = jnp.zeros_like(wet_here)
            total_u = total_v = low_u = low_v = zero

            def fetch(level):
                if level == levels:
                    return zero, zero
                u = source[1 + level, source_at]
                v = source[1 + levels + level, source_at]
                if first:
                    u = jnp.where(wet_here > level, u, 0.0)
                    v = jnp.where(wet_here > level, v, 0.0)
                return u, v

            u_up = v_up = zero
            u, v = fetch(0)
            for level in range(levels):
                u_down, v_down = fetch(level + 1)
                inside = wet_here > level + 1
                bottom = wet_here == level + 1
                own = 1.0 if level == 0 else 0.9
                weight = jnp.where(inside, own - 0.1, own)
                retain = jnp.where(inside, 1.0, jnp.where(bottom, slow, 0.0))
                ut = weight * u + 0.1 * (v + u_up + u_down) - grad_x
                vt = weight * v + 0.1 * (v_up + v_down - u) - grad_y
                low_u = jnp.where(bottom, ut, low_u)
                low_v = jnp.where(bottom, vt, low_v)
                u_new = ut * retain
                v_new = vt * retain
                if into_final:
                    final[1 + level, source_at] = u_new
                    final[1 + levels + level, source_at] = v_new
                else:
                    work[1 + level, at] = u_new
                    work[1 + levels + level, at] = v_new
                    total_u += u_new
                    total_v += v_new
                u_up, v_up, u, v = u, v, u_down, v_down
            sum_u[at] = total_u
            sum_v[at] = total_v
            bot_u[at] = low_u
            bot_v[at] = low_v

        if first:
            over_blocks(rows, REACH, update, state, above, below)
        elif last:

            def into_final(start):
                at = pl.ds(pl.multiple_of(start + REACH, BLOCK), BLOCK)
                update(at, Shifted(work, at), pl.ds(start, BLOCK), True)

            looped(rows, into_final)
            for start in range(HALO, REACH, BLOCK):
                for at in (pl.ds(start, BLOCK), pl.ds(start + HALO + rows, BLOCK)):
                    update(at, work, at)
        else:

            def in_place(start):
                at = pl.ds(start, BLOCK)
                update(at, work, at)

            looped(rows + 2 * REACH, in_place)
        saved[2 + 2 * step] = bot_u[HALO : REACH + HALO + rows]
        saved[3 + 2 * step] = bot_v[HALO : REACH + HALO + rows]
        bot_u[...] = factor[...] * bot_u[...]
        bot_v[...] = factor[...] * bot_v[...]
    final[0] = eta[REACH : REACH + rows]
    pack(final, wet, order, packed)


def adjoint_kernel(adjoint, misfit, kept, above, below, depth, wet, drag,
                   start, gradient,
                   work, wet_pad, thick, drag_pad, eta, sum_u, sum_v, bot_u, bot_v,
                   push_x, push_y, push_low_x, push_low_y, factor, grad_pad):
    fields, rows, _ = adjoint.shape
    levels = (fields - 1) // 2
    fill_padded(wet_pad, wet[...], above[fields + 1, HALO:], below[fields + 1, :HALO])
    fill_padded(drag_pad, drag[...], above[fields + 2, HALO:], below[fields + 2, :HALO])
    fill_padded(thick, depth[...], above[fields, HALO:], below[fields, :HALO])
    above = AdjointEdge(above, fields)
    below = AdjointEdge(below, fields)
    thick[...] = thick[...] / jnp.maximum(wet_pad[...], 1.0)
    fill_padded(eta, adjoint[0], above[0, :], below[0, :])
    grad_pad[...] = jnp.zeros_like(grad_pad)
    sea = jnp.minimum(wet_pad[...], 1.0)

    before = [(kept[0], kept[1])]
    for step in range(STEPS - 1):
        slow = drag_terms(*before[step], thick[...], drag_pad[...], sea)[2]
        before.append((slow * kept[2 + 2 * step], slow * kept[3 + 2 * step]))

    def sums(at, source, source_at):
        wet_here = wet_pad[at]
        total_u = total_v = low_u = low_v = jnp.zeros_like(wet_here)
        for level in range(levels):
            active = wet_here > level
            bottom = wet_here == level + 1
            u = jnp.where(active, source[1 + level, source_at], 0.0)
            v = jnp.where(active, source[1 + levels + level, source_at], 0.0)
            total_u += u
            total_v += v
            low_u = jnp.where(bottom, u, low_u)
            low_v = jnp.where(bottom, v, low_v)
        sum_u[at] = total_u
        sum_v[at] = total_v
        bot_u[at] = low_u
        bot_v[at] = low_v

    over_blocks(rows, HALO, sums, adjoint, above, below)

    for step in reversed(range(STEPS)):
        first, last = step == STEPS - 1, step == 0
        sea = jnp.minimum(wet_pad[...], 1.0)
        fill_padded(push_x, misfit[step], above[fields + step, :], below[fields + step, :])
        u_before, v_before = before[step]
        speed, denominator, slow = drag_terms(u_before, v_before, thick[...], drag_pad[...], sea)
        factor[...] = slow
        low_u, low_v = bot_u[...], bot_v[...]
        on_factor = low_u * kept[2 + 2 * step] + low_v * kept[3 + 2 * step]
        on_denominator = -on_factor * slow / denominator
        grad_pad[...] += 0.1 * speed * on_denominator
        on_speed = 0.1 * drag_pad[...] * on_denominator / speed
        loss = 1.0 - slow
        total_x = sum_u[...] - loss * low_u
        total_y = sum_v[...] - loss * low_v
        surface = sea * (eta[...] + push_x[...] + 0.2 * (row_diff(total_x) + column_diff(total_y)))
        eta[...] = surface
        thin = 0.2 * thick[...]
        toward_x = thin * row_diff(surface)
        toward_y = thin * column_diff(surface)
        push_x[...] = toward_x
        push_y[...] = toward_y
        push_low_x[...] = toward_x + on_speed * u_before
        push_low_y[...] = toward_y + on_speed * v_before

        def update(at, source, source_at, offset=0):
            if offset:
                at = source.at
            wet_here = wet_pad[at]
            slow_here = factor[at]
            along_x, along_y = push_x[at], push_y[at]
            low_x, low_y = push_low_x[at], push_low_y[at]
            zero = jnp.zeros_like(wet_here)
            total_u = total_v = low_u = low_v = zero

            def fetch(level):
                if level == levels:
                    return zero, zero
                retain = jnp.where(wet_here > level + 1, 1.0, jnp.where(wet_here > level, slow_here, 0.0))
                return retain * source[1 + level, source_at], retain * source[1 + levels + level, source_at]

            p_up = q_up = zero
            p, q = fetch(0)
            for level in range(levels):
                p_down, q_down = fetch(level + 1)
                inside = wet_here > level + 1
                bottom = wet_here == level + 1
                active = wet_here > level
                own = 1.0 if level == 0 else 0.9
                weight = jnp.where(inside, own - 0.1, own)
                u = weight * p + 0.1 * (p_up + p_down - q) + jnp.where(inside, along_x, low_x)
                v = weight * q + 0.1 * (q_up + q_down + p) + jnp.where(inside, along_y, low_y)
                u = jnp.where(active, u, 0.0)
                v = jnp.where(active, v, 0.0)
                if last:
                    start[1 + level, source_at] = u
                    start[1 + levels + level, source_at] = v
                else:
                    work[1 + level, at] = u
                    work[1 + levels + level, at] = v
                    total_u += u
                    total_v += v
                    low_u = jnp.where(bottom, u, low_u)
                    low_v = jnp.where(bottom, v, low_v)
                p_up, q_up, p, q = p, q, p_down, q_down
            if not last:
                sum_u[at] = total_u
                sum_v[at] = total_v
                bot_u[at] = low_u
                bot_v[at] = low_v

        if first:
            over_blocks(rows, HALO, update, adjoint, above, below)
        elif last:

            def into_start(begin):
                update(pl.ds(begin, BLOCK), Shifted(work, pl.ds(pl.multiple_of(begin + HALO, BLOCK), BLOCK)),
                       pl.ds(begin, BLOCK), HALO)

            looped(rows, into_start)
        else:

            def in_place(begin):
                at = pl.ds(begin, BLOCK)
                update(at, work, at)

            looped(rows + 2 * HALO, in_place)
    start[0] = eta[HALO : HALO + rows]
    gradient[...] = grad_pad[HALO : HALO + rows]


def body(start_states, end_adjoints, misfits, water_depth, drag_coef, sea_mask, bottom_level):
    initial = start_states[0]
    adjoint = end_adjoints[0]
    misfit = misfits[0]
    fields, rows, width = initial.shape
    floats = lambda *shape: jax.ShapeDtypeStruct(shape, jnp.float32)
    whole_numbers = lambda *shape: jax.ShapeDtypeStruct(shape, jnp.int32)
    pad = lambda halo: pltpu.VMEM((rows + 2 * halo, width), jnp.float32)
    work = lambda halo: pltpu.VMEM((fields, rows + 2 * halo, width), jnp.float32)
    params = pltpu.CompilerParams(vmem_limit_bytes=32 << 20)
    cells = fields * rows * width
    cost = pl.CostEstimate(flops=100 * cells, bytes_accessed=10 * cells, transcendentals=0)
    state_shape = floats(fields, rows, width)
    packed_shape = floats(2 * SLOTS + 2, rows // 2, width)
    edge_shape = floats(edge_planes(fields), REACH, width)
    in_vmem = pl.BlockSpec(memory_space=pltpu.VMEM)
    in_smem = pl.BlockSpec(memory_space=pltpu.SMEM)
    anywhere = pl.BlockSpec(memory_space=pl.ANY)

    upward, downward = pl.pallas_call(
        edge_kernel,
        in_specs=[anywhere] * 2 + [in_vmem] * 5,
        out_shape=(edge_shape, edge_shape),
        scratch_shapes=[pltpu.SemaphoreType.DMA((6,))],
        cost_estimate=cost,
        name="edges",
    )(initial, adjoint, misfit, water_depth, drag_coef, sea_mask, bottom_level)
    above = shifted(downward, "tile", 1)
    below = shifted(upward, "tile", -1)

    wet, order, place, deepest = pl.pallas_call(
        plan_kernel,
        out_specs=(in_vmem,) * 3 + (in_smem,),
        out_shape=(floats(rows, width), whole_numbers(rows, width), whole_numbers(rows, width), whole_numbers(1, 1)),
        cost_estimate=cost,
        name="plan",
    )(sea_mask, bottom_level)

    final, saved, final_packed = pl.pallas_call(
        forward_kernel,
        out_shape=(state_shape, floats(SAVED, rows + 2 * HALO, width), packed_shape),
        scratch_shapes=[work(REACH)] + [pad(REACH)] * 11,
        compiler_params=params,
        cost_estimate=cost,
        name="forward",
    )(initial, above, below, water_depth, wet, drag_coef, order)
    came_state = passed_along(final_packed, "slab", 1)

    start, gradient = pl.pallas_call(
        adjoint_kernel,
        out_shape=(state_shape, floats(rows, width)),
        scratch_shapes=[work(HALO)] + [pad(HALO)] * 14,
        compiler_params=params,
        cost_estimate=cost,
        name="adjoint",
    )(adjoint, misfit, saved, above, below, water_depth, wet, drag_coef)
    slabs = lax.axis_size("slab")
    if slabs > 4:
        gradients = [lax.psum(gradient, "slab")]
    else:
        gradients = [gradient] + [passed_along(gradient, "slab", distance) for distance in range(1, slabs)]
    start_packed = pl.pallas_call(
        pack_kernel, out_shape=packed_shape, compiler_params=params, cost_estimate=cost, name="pack"
    )(start, wet, order)
    came_adjoint = passed_along(start_packed, "slab", -1)

    def received(kernel, packed, sent, distance, *extra):
        fallback = lax.cond(
            deepest[0, 0] > SLOTS,
            lambda sent: passed_along(sent, "slab", distance),
            lambda sent: pl.pallas_call(nothing_kernel, out_specs=anywhere, out_shape=state_shape, name="nothing")(),
            sent,
        )
        pool = pl.BlockSpec((POOL, width), lambda i: (i, 0))
        return pl.pallas_call(
            kernel,
            grid=(rows // POOL,),
            in_specs=[in_smem, pl.BlockSpec((2 * SLOTS + 2, POOL // 2, width), lambda i: (0, i, 0)),
                      pool, pool, pool, anywhere] + [pool] * len(extra),
            out_specs=[pl.BlockSpec((fields, POOL, width), lambda i: (0, i, 0))] + [pool] * bool(extra),
            out_shape=[state_shape] + [floats(rows, width)] * bool(extra),
            compiler_params=params,
            cost_estimate=cost,
            name="unpack",
        )(deepest, packed, wet, order, place, fallback, *extra)

    (next_state,) = received(unpack_kernel, came_state, final, 1)
    next_adjoint, drag_total = received(unpack_adjoint_kernel, came_adjoint, start, -1, *gradients)
    return (next_state[None], next_adjoint[None], drag_total)


def solution(mesh):
    return jax.shard_map(
        body,
        mesh=mesh,
        in_specs=(
            P(("groups", "slab"), None, "tile", None),
            P(("groups", "slab"), None, "tile", None),
            P(("groups", "slab"), None, "tile", None),
            P(("groups", "tile"), None),
            P(("groups", "tile"), None),
            P(("groups", "tile"), None),
            P(("groups", "tile"), None),
        ),
        out_specs=(
            P(("groups", "slab"), None, "tile", None),
            P(("groups", "slab"), None, "tile", None),
            P(("groups", "tile"), None),
        ),
        check_vma=False,
    )
```

```python
import jax
import jax.numpy as jnp
from jax import lax
from jax.experimental import pallas as pl
from jax.experimental.pallas import tpu as pltpu
from jax.sharding import PartitionSpec as P

STEPS = 4
BLOCK = 8
HALO = 2 * STEPS
REACH = 2 * HALO
SAVED = 2 + 2 * STEPS
POOL = 4 * BLOCK
SLOTS = 29


def shifted(block, axis, distance):
    devices = range(lax.axis_size(axis))
    route = [(i - distance, i) for i in devices if i - distance in devices]
    return lax.ppermute(block, axis, route)


def passed_along(block, axis, distance):
    devices = range(lax.axis_size(axis))
    route = [((i - distance) % len(devices), i) for i in devices]
    return lax.ppermute(block, axis, route)


def row_diff(values):
    return pltpu.roll(values, values.shape[0] - 1, 0) - pltpu.roll(values, 1, 0)


def column_diff(values):
    width = values.shape[1]
    lane = lax.broadcasted_iota(jnp.int32, values.shape, 1)
    after = jnp.where(lane < width - 1, pltpu.roll(values, width - 1, 1), 0.0)
    before = jnp.where(lane > 0, pltpu.roll(values, 1, 1), 0.0)
    return after - before


def looped(count, visit):
    def one(index, carry):
        visit(pl.multiple_of(index * BLOCK, BLOCK))
        return carry

    lax.fori_loop(0, count // BLOCK, one, 0)


def over_blocks(rows, halo, visit, own, above, below):
    block = lambda start: pl.ds(start if isinstance(start, int) else pl.multiple_of(start, BLOCK), BLOCK)
    looped(halo, lambda start: visit(block(start), above, block(start)))
    looped(rows, lambda start: visit(block(start + halo), own, block(start)))
    looped(halo, lambda start: visit(block(start + halo + rows), below, block(start)))


def fill_padded(target, own, above, below):
    rows, halo = own.shape[0], above.shape[0]
    target[0:halo] = above
    target[halo : halo + rows] = own
    target[halo + rows : rows + 2 * halo] = below


class Shifted:
    def __init__(self, ref, at):
        self.ref, self.at = ref, at

    def __getitem__(self, key):
        return self.ref[key[0], self.at]


class AdjointEdge:
    def __init__(self, ref, fields):
        self.ref, self.fields = ref, fields

    def __getitem__(self, key):
        plane, rows = edge_place(self.fields, key[0])
        return self.ref[plane, rows]


def edge_planes(fields):
    return fields + 3 + (fields + STEPS + 1) // 2


def edge_place(fields, item):
    first = (fields + STEPS + 1) // 2
    half = 0 if item < first else HALO
    return fields + 3 + item - (first if half else 0), pl.ds(half, HALO)


def lanes_of(values):
    return lax.broadcasted_iota(jnp.int32, values.shape, values.ndim - 1)


def take_lanes(values, index):
    return jnp.take_along_axis(values, index, axis=1, mode="promise_in_bounds")


def plan_kernel(mask, bottom, wet, order, place, deepest):
    rows, width = mask.shape
    half = width // 2
    depth = mask[...] * bottom[...]
    wet[...] = depth.astype(jnp.float32)
    lane = lanes_of(depth)
    even = (lax.broadcasted_iota(jnp.int32, depth.shape, 0) // BLOCK) % 2 == 0
    key = (depth * width + lane).astype(jnp.float32)
    rank = jnp.zeros_like(depth)
    for shift in range(1, width):
        rank = rank + jnp.where(pltpu.roll(key, shift, 1) > key, 1, 0)
    ahead = jnp.where(rank < half, rank, width + half - 1 - rank)
    behind = jnp.where(rank < half, rank + half, width - 1 - rank)
    there = jnp.where(even, ahead, behind)
    place[...] = there
    moved = jnp.zeros_like(depth)
    for shift in range(1, width):
        moved = jnp.where(pltpu.roll(there, shift, 1) == lane, shift, moved)
    origin = (lane - moved) & (width - 1)
    order[...] = origin
    most = jnp.zeros((BLOCK, width), jnp.float32)
    for pool in range(rows // POOL):
        ats = [slice(pool * POOL + block * BLOCK, pool * POOL + (block + 1) * BLOCK) for block in range(4)]
        deep, shallow, swap = pair_up([take_lanes(wet[at], origin[at]) for at in ats])
        most = jnp.maximum(most, deep[0] + jnp.where(swap, shallow[1], shallow[0]))
        most = jnp.maximum(most, deep[1] + jnp.where(swap, shallow[0], shallow[1]))
    deepest[0, 0] = jnp.max(most).astype(jnp.int32)


def deep_and_shallow(blocks):
    first = lanes_of(blocks[0]) < blocks[0].shape[1] // 2
    deep = [jnp.where(first, blocks[0], blocks[1]), jnp.where(first, blocks[2], blocks[3])]
    shallow = [jnp.where(first, blocks[1], blocks[0]), jnp.where(first, blocks[3], blocks[2])]
    return deep, shallow


def pair_up(depths):
    deep, shallow = deep_and_shallow(depths)
    swap = (deep[0] - deep[1]) * (shallow[0] - shallow[1]) > 0.0
    return deep, shallow, swap


def pool_rows(pool):
    start = pl.multiple_of(pool * POOL, POOL)
    return [pl.ds(pl.multiple_of(start + block * BLOCK, BLOCK), BLOCK) for block in range(4)]


def pool_slots(pool):
    start = pl.multiple_of(pool * (POOL // 2), POOL // 2)
    return [pl.ds(pl.multiple_of(start + block * BLOCK, BLOCK), BLOCK) for block in range(2)]


def pack(state, wet, order, packed):
    levels = (state.shape[0] - 1) // 2

    def one_pool(pool, carry):
        ats = pool_rows(pool)
        slots = pool_slots(pool)
        orders = [order[at, :] for at in ats]
        deep_wet, _, swap = pair_up([take_lanes(wet[at, :], by) for at, by in zip(ats, orders)])
        for base, target in ((1, 0), (1 + levels, SLOTS)):

            def sorted_level(level):
                parts = [take_lanes(state[base + level, at, :], by) for at, by in zip(ats, orders)]
                deep, shallow = deep_and_shallow(parts)
                return deep, (jnp.where(swap, shallow[1], shallow[0]), jnp.where(swap, shallow[0], shallow[1]))

            for near in range((SLOTS + 1) // 2):
                far = SLOTS - 1 - near
                both = far < levels
                deep, shallow = sorted_level(near)
                far_deep, far_shallow = sorted_level(far) if both and far > near else (deep, shallow)
                for half in range(2):
                    value = deep[half]
                    if both:
                        value = jnp.where(deep_wet[half] > near, value, far_shallow[half])
                    packed[target + near, slots[half], :] = value
                    if far > near:
                        value = shallow[half]
                        if both:
                            value = jnp.where(deep_wet[half] > far, far_deep[half], value)
                        packed[target + far, slots[half], :] = value
        return carry

    lax.fori_loop(0, packed.shape[1] // (POOL // 2), one_pool, 0)


def pack_kernel(state, wet, order, packed):
    pack(state, wet, order, packed)


def unpack_pool(packed, wet, order, place, state, pool):
    levels = (state.shape[0] - 1) // 2
    ats = pool_rows(pool)
    slots = pool_slots(pool)
    wets = [wet[at, :] for at in ats]
    places = [place[at, :] for at in ats]
    _, _, swap = pair_up([take_lanes(depth, order[at, :]) for depth, at in zip(wets, ats)])
    first = lanes_of(swap) < swap.shape[1] // 2
    for base, source in ((1, 0), (1 + levels, SLOTS)):

        def write_level(level, deep, ends):
            shallow = jnp.where(swap, ends[1], ends[0]), jnp.where(swap, ends[0], ends[1])
            for block in range(4):
                pair = deep[block // 2], shallow[block // 2]
                if block % 2:
                    pair = pair[::-1]
                value = take_lanes(jnp.where(first, *pair), places[block])
                state[base + level, ats[block], :] = jnp.where(wets[block] > level, value, 0.0)

        for near in range((SLOTS + 1) // 2):
            far = SLOTS - 1 - near
            head = [packed[source + near, slot, :] for slot in slots]
            tail = [packed[source + far, slot, :] for slot in slots]
            write_level(near, head, tail)
            if near < far < levels:
                write_level(far, tail, head)


def unpack_kernel(deepest, packed, wet, order, place, whole, *rest):
    *gradients, state, total = rest
    pool = pl.program_id(0)

    @pl.when(deepest[0, 0] > SLOTS)
    def _():
        pltpu.sync_copy(whole.at[:, pl.ds(pl.multiple_of(pool * POOL, POOL), POOL), :], state)

    @pl.when(deepest[0, 0] <= SLOTS)
    def _():
        unpack_pool(packed, wet, order, place, state, 0)
        for half in range(2):
            state[0, half * (POOL // 2) : (half + 1) * (POOL // 2)] = packed[2 * SLOTS + half]

    summed = gradients[0][...]
    for gradient in gradients[1:]:
        summed = summed + gradient[...]
    total[...] = summed


def replay_kernel(deepest, packed, wet, order, place, depth, drag, surfaces, whole, final,
                  thick, bot_u, bot_v, slope_x, slope_y, factor):
    fields, rows, width = final.shape
    levels = (fields - 1) // 2

    @pl.when(deepest[0, 0] > SLOTS)
    def _():
        pltpu.sync_copy(whole, final)
        for level in range(levels):
            active = wet[...] > level
            for at in (1 + level, 1 + levels + level):
                final[at] = jnp.where(active, final[at], 0.0)

    @pl.when(deepest[0, 0] <= SLOTS)
    def _():
        def one_pool(pool, carry):
            unpack_pool(packed, wet, order, place, final, pool)
            return carry

        lax.fori_loop(0, rows // POOL, one_pool, 0)

    def lowest(start):
        at = pl.ds(start, BLOCK)
        wet_here = wet[at, :]
        low_u = low_v = jnp.zeros_like(wet_here)
        for level in range(levels):
            bottom = wet_here == level + 1
            low_u = jnp.where(bottom, final[1 + level, at, :], low_u)
            low_v = jnp.where(bottom, final[1 + levels + level, at, :], low_v)
        bot_u[at, :] = low_u
        bot_v[at, :] = low_v

    looped(rows, lowest)
    sea = jnp.minimum(wet[...], 1.0)
    thick[...] = depth[...] / jnp.maximum(wet[...], 1.0)
    for step in range(STEPS):
        surface = surfaces[step]
        slope_x[...] = 0.2 * row_diff(surface)[HALO : HALO + rows]
        slope_y[...] = 0.2 * column_diff(surface[HALO : HALO + rows])
        factor[...] = drag_terms(bot_u[...], bot_v[...], thick[...], drag[...], sea)[2]

        def update(start):
            at = pl.ds(start, BLOCK)

            def store(level, u, v):
                final[1 + level, at, :] = u
                final[1 + levels + level, at, :] = v

            slow = factor[at, :]
            fetch = lambda level: (final[1 + level, at, :], final[1 + levels + level, at, :])
            _, low, _ = column_step(levels, wet[at, :], slow, slope_x[at, :], slope_y[at, :], fetch, store)
            bot_u[at, :] = slow * low[0]
            bot_v[at, :] = slow * low[1]

        looped(rows, update)
    final[0] = surfaces[STEPS - 1, HALO : HALO + rows]


def edge_kernel(state, adjoint, misfit, depth, drag, mask, bottom, upward, downward, sea_rows, level_rows, sems):
    fields, rows, _ = state.shape
    first = (fields + STEPS + 1) // 2
    joint = fields + 3
    copies = []

    def bring(source, target):
        copies.append(pltpu.make_async_copy(source, target, sems.at[len(copies)]))

    for side, target in enumerate((upward, downward)):
        wide = pl.ds(side * (rows - REACH), REACH)
        narrow = pl.ds(side * (rows - HALO), HALO)
        bring(state.at[:, wide, :], target.at[pl.ds(0, fields)])
        bring(adjoint.at[pl.ds(0, first), narrow, :], target.at[pl.ds(joint, first), pl.ds(0, HALO), :])
        bring(
            adjoint.at[pl.ds(first, fields - first), narrow, :],
            target.at[pl.ds(joint, fields - first), pl.ds(HALO, HALO), :],
        )
        for step in range(STEPS):
            plane, at = edge_place(fields, fields + step)
            bring(misfit.at[step, narrow, :], target.at[plane, at, :])
        bring(depth.at[wide, :], target.at[fields])
        bring(drag.at[wide, :], target.at[fields + 2])
        bring(mask.at[wide, :], sea_rows.at[side])
        bring(bottom.at[wide, :], level_rows.at[side])
    for copy in copies:
        copy.start()
    for copy in copies:
        copy.wait()
    for side, target in enumerate((upward, downward)):
        target[fields + 1] = (sea_rows[side] * level_rows[side]).astype(jnp.float32)


def nothing_kernel(result):
    pass


def drag_terms(u_bottom, v_bottom, thickness, drag, sea):
    speed = jnp.sqrt(u_bottom * u_bottom + v_bottom * v_bottom + 0.0025)
    denominator = thickness + 0.1 * drag * speed + 1.0 - sea
    return speed, denominator, thickness / denominator


def column_step(levels, wet_here, slow, grad_x, grad_y, fetch, store):
    zero = jnp.zeros_like(wet_here)
    total = low = second = (zero, zero)
    u_up = v_up = zero
    u, v = fetch(0)
    for level in range(levels):
        u_down, v_down = fetch(level + 1) if level + 1 < levels else (zero, zero)
        inside = wet_here > level + 1
        bottom = wet_here == level + 1
        above_bottom = wet_here == level + 2
        own = 1.0 if level == 0 else 0.9
        weight = jnp.where(inside, own - 0.1, own)
        retain = jnp.where(inside, 1.0, jnp.where(bottom, slow, 0.0))
        ut = weight * u + 0.1 * (v + u_up + u_down) - grad_x
        vt = weight * v + 0.1 * (v_up + v_down - u) - grad_y
        low = jnp.where(bottom, ut, low[0]), jnp.where(bottom, vt, low[1])
        u_new = ut * retain
        v_new = vt * retain
        second = jnp.where(above_bottom, u_new, second[0]), jnp.where(above_bottom, v_new, second[1])
        store(level, u_new, v_new)
        total = total[0] + u_new, total[1] + v_new
        u_up, v_up, u, v = u, v, u_down, v_down
    return total, low, second


def forward_kernel(state, above, below, depth, wet, drag, saved, surfaces,
                   work, wet_pad, thick, drag_pad, eta, sum_u, sum_v, bot_u, bot_v, next_u, next_v,
                   slope_x, slope_y, factor):
    fields, rows, _ = state.shape
    levels = (fields - 1) // 2
    kept_rows = slice(HALO, REACH + HALO + rows)
    fill_padded(wet_pad, wet[...], above[fields + 1], below[fields + 1])
    fill_padded(drag_pad, drag[...], above[fields + 2], below[fields + 2])
    fill_padded(thick, depth[...], above[fields], below[fields])
    fill_padded(eta, state[0], above[0], below[0])
    thick[...] = thick[...] / jnp.maximum(wet_pad[...], 1.0)

    def sums(at, source, source_at):
        wet_here = wet_pad[at]
        total_u = total_v = low_u = low_v = jnp.zeros_like(wet_here)
        for level in range(levels):
            active = wet_here > level
            bottom = wet_here == level + 1
            u = jnp.where(active, source[1 + level, source_at], 0.0)
            v = jnp.where(active, source[1 + levels + level, source_at], 0.0)
            total_u += u
            total_v += v
            low_u = jnp.where(bottom, u, low_u)
            low_v = jnp.where(bottom, v, low_v)
        sum_u[at] = total_u
        sum_v[at] = total_v
        bot_u[at] = low_u
        bot_v[at] = low_v

    over_blocks(rows, REACH, sums, state, above, below)
    saved[0] = bot_u[kept_rows]
    saved[1] = bot_v[kept_rows]

    for step in range(STEPS):
        sea = jnp.minimum(wet_pad[...], 1.0)
        flux_x = thick[...] * sum_u[...]
        flux_y = thick[...] * sum_v[...]
        surface = sea * (eta[...] - 0.2 * (row_diff(flux_x) + column_diff(flux_y)))
        eta[...] = surface
        surfaces[step] = eta[kept_rows]
        slope_x[...] = 0.2 * row_diff(surface)
        slope_y[...] = 0.2 * column_diff(surface)
        if step == STEPS - 1:
            weight = jnp.where(wet_pad[...] > 1.0, 0.9, 1.0)
            low_u, low_v = bot_u[...], bot_v[...]
            floor = wet_pad[...] > 0.0
            last_u = weight * low_u + 0.1 * (low_v + next_u[...]) - slope_x[...]
            last_v = weight * low_v + 0.1 * (next_v[...] - low_u) - slope_y[...]
            bot_u[...] = jnp.where(floor, last_u, 0.0)
            bot_v[...] = jnp.where(floor, last_v, 0.0)
        else:
            factor[...] = drag_terms(bot_u[...], bot_v[...], thick[...], drag_pad[...], sea)[2]

            def update(at, source, source_at):
                wet_here = wet_pad[at]

                def fetch(level):
                    u = source[1 + level, source_at]
                    v = source[1 + levels + level, source_at]
                    if step == 0:
                        u = jnp.where(wet_here > level, u, 0.0)
                        v = jnp.where(wet_here > level, v, 0.0)
                    return u, v

                def store(level, u, v):
                    work[1 + level, at] = u
                    work[1 + levels + level, at] = v

                total, low, second = column_step(
                    levels, wet_here, factor[at], slope_x[at], slope_y[at], fetch, store
                )
                sum_u[at], sum_v[at] = total
                bot_u[at], bot_v[at] = low
                next_u[at], next_v[at] = second

            if step == 0:
                over_blocks(rows, REACH, update, state, above, below)
            else:
                looped(rows + 2 * REACH, lambda start: update(pl.ds(start, BLOCK), work, pl.ds(start, BLOCK)))
        saved[2 + 2 * step] = bot_u[kept_rows]
        saved[3 + 2 * step] = bot_v[kept_rows]
        if step < STEPS - 1:
            bot_u[...] = factor[...] * bot_u[...]
            bot_v[...] = factor[...] * bot_v[...]


def adjoint_kernel(adjoint, misfit, kept, above, below, depth, wet, drag, order,
                   output, gradient, packed, start, sem,
                   work, wet_pad, thick, drag_pad, eta, sum_u, sum_v, bot_u, bot_v,
                   push_x, push_y, push_low_x, push_low_y, factor, grad_pad):
    fields, rows, _ = adjoint.shape
    levels = (fields - 1) // 2
    fill_padded(wet_pad, wet[...], above[fields + 1, HALO:], below[fields + 1, :HALO])
    fill_padded(drag_pad, drag[...], above[fields + 2, HALO:], below[fields + 2, :HALO])
    fill_padded(thick, depth[...], above[fields, HALO:], below[fields, :HALO])
    above = AdjointEdge(above, fields)
    below = AdjointEdge(below, fields)
    thick[...] = thick[...] / jnp.maximum(wet_pad[...], 1.0)
    fill_padded(eta, adjoint[0], above[0, :], below[0, :])
    grad_pad[...] = jnp.zeros_like(grad_pad)
    sea = jnp.minimum(wet_pad[...], 1.0)

    before = [(kept[0], kept[1])]
    for step in range(STEPS - 1):
        slow = drag_terms(*before[step], thick[...], drag_pad[...], sea)[2]
        before.append((slow * kept[2 + 2 * step], slow * kept[3 + 2 * step]))

    def sums(at, source, source_at):
        wet_here = wet_pad[at]
        total_u = total_v = low_u = low_v = jnp.zeros_like(wet_here)
        for level in range(levels):
            active = wet_here > level
            bottom = wet_here == level + 1
            u = jnp.where(active, source[1 + level, source_at], 0.0)
            v = jnp.where(active, source[1 + levels + level, source_at], 0.0)
            total_u += u
            total_v += v
            low_u = jnp.where(bottom, u, low_u)
            low_v = jnp.where(bottom, v, low_v)
        sum_u[at] = total_u
        sum_v[at] = total_v
        bot_u[at] = low_u
        bot_v[at] = low_v

    over_blocks(rows, HALO, sums, adjoint, above, below)

    for step in reversed(range(STEPS)):
        first, last = step == STEPS - 1, step == 0
        sea = jnp.minimum(wet_pad[...], 1.0)
        fill_padded(push_x, misfit[step], above[fields + step, :], below[fields + step, :])
        u_before, v_before = before[step]
        speed, denominator, slow = drag_terms(u_before, v_before, thick[...], drag_pad[...], sea)
        factor[...] = slow
        low_u, low_v = bot_u[...], bot_v[...]
        on_factor = low_u * kept[2 + 2 * step] + low_v * kept[3 + 2 * step]
        on_denominator = -on_factor * slow / denominator
        grad_pad[...] += 0.1 * speed * on_denominator
        on_speed = 0.1 * drag_pad[...] * on_denominator / speed
        loss = 1.0 - slow
        total_x = sum_u[...] - loss * low_u
        total_y = sum_v[...] - loss * low_v
        surface = sea * (eta[...] + push_x[...] + 0.2 * (row_diff(total_x) + column_diff(total_y)))
        eta[...] = surface
        thin = 0.2 * thick[...]
        toward_x = thin * row_diff(surface)
        toward_y = thin * column_diff(surface)
        push_x[...] = toward_x
        push_y[...] = toward_y
        push_low_x[...] = toward_x + on_speed * u_before
        push_low_y[...] = toward_y + on_speed * v_before

        def update(at, source, source_at, offset=0):
            if offset:
                at = source.at
            wet_here = wet_pad[at]
            slow_here = factor[at]
            along_x, along_y = push_x[at], push_y[at]
            low_x, low_y = push_low_x[at], push_low_y[at]
            zero = jnp.zeros_like(wet_here)
            total_u = total_v = low_u = low_v = zero

            def fetch(level):
                if level == levels:
                    return zero, zero
                retain = jnp.where(wet_here > level + 1, 1.0, jnp.where(wet_here > level, slow_here, 0.0))
                return retain * source[1 + level, source_at], retain * source[1 + levels + level, source_at]

            p_up = q_up = zero
            p, q = fetch(0)
            for level in range(levels):
                p_down, q_down = fetch(level + 1)
                inside = wet_here > level + 1
                bottom = wet_here == level + 1
                active = wet_here > level
                own = 1.0 if level == 0 else 0.9
                weight = jnp.where(inside, own - 0.1, own)
                u = weight * p + 0.1 * (p_up + p_down - q) + jnp.where(inside, along_x, low_x)
                v = weight * q + 0.1 * (q_up + q_down + p) + jnp.where(inside, along_y, low_y)
                u = jnp.where(active, u, 0.0)
                v = jnp.where(active, v, 0.0)
                if last:
                    start[1 + level, source_at] = u
                    start[1 + levels + level, source_at] = v
                else:
                    work[1 + level, at] = u
                    work[1 + levels + level, at] = v
                    total_u += u
                    total_v += v
                    low_u = jnp.where(bottom, u, low_u)
                    low_v = jnp.where(bottom, v, low_v)
                p_up, q_up, p, q = p, q, p_down, q_down
            if not last:
                sum_u[at] = total_u
                sum_v[at] = total_v
                bot_u[at] = low_u
                bot_v[at] = low_v

        if first:
            over_blocks(rows, HALO, update, adjoint, above, below)
        elif last:

            def into_start(begin):
                update(pl.ds(begin, BLOCK), Shifted(work, pl.ds(pl.multiple_of(begin + HALO, BLOCK), BLOCK)),
                       pl.ds(begin, BLOCK), HALO)

            looped(rows, into_start)
        else:

            def in_place(begin):
                at = pl.ds(begin, BLOCK)
                update(at, work, at)

            looped(rows + 2 * HALO, in_place)
    start[0] = eta[HALO : HALO + rows]
    gradient[...] = grad_pad[HALO : HALO + rows]
    copy = pltpu.make_async_copy(start, output, sem)
    copy.start()
    pack(start, wet, order, packed)
    for pool in range(rows // POOL):
        for half in range(2):
            at = pool * POOL + half * (POOL // 2)
            packed[2 * SLOTS + half, pool * (POOL // 2) : (pool + 1) * (POOL // 2)] = start[0, at : at + POOL // 2]
    copy.wait()


def body(start_states, end_adjoints, misfits, water_depth, drag_coef, sea_mask, bottom_level):
    initial = start_states[0]
    adjoint = end_adjoints[0]
    misfit = misfits[0]
    fields, rows, width = initial.shape
    floats = lambda *shape: jax.ShapeDtypeStruct(shape, jnp.float32)
    whole_numbers = lambda *shape: jax.ShapeDtypeStruct(shape, jnp.int32)
    pad = lambda halo: pltpu.VMEM((rows + 2 * halo, width), jnp.float32)
    work = lambda halo: pltpu.VMEM((fields, rows + 2 * halo, width), jnp.float32)
    params = pltpu.CompilerParams(vmem_limit_bytes=16 << 20)
    cells = fields * rows * width
    cost = pl.CostEstimate(flops=100 * cells, bytes_accessed=10 * cells, transcendentals=0)
    state_shape = floats(fields, rows, width)
    packed_shape = floats(2 * SLOTS + 2, rows // 2, width)
    edge_shape = floats(edge_planes(fields), REACH, width)
    in_vmem = pl.BlockSpec(memory_space=pltpu.VMEM)
    in_smem = pl.BlockSpec(memory_space=pltpu.SMEM)
    anywhere = pl.BlockSpec(memory_space=pl.ANY)

    upward, downward = pl.pallas_call(
        edge_kernel,
        in_specs=[anywhere] * 7,
        out_specs=(in_vmem, in_vmem),
        out_shape=(edge_shape, edge_shape),
        scratch_shapes=[pltpu.VMEM((2, REACH, width), jnp.int32)] * 2 + [pltpu.SemaphoreType.DMA((22,))],
        compiler_params=params,
        cost_estimate=cost,
        name="edges",
    )(initial, adjoint, misfit, water_depth, drag_coef, sea_mask, bottom_level)
    above = shifted(downward, "tile", 1)
    below = shifted(upward, "tile", -1)

    wet, order, place, deepest = pl.pallas_call(
        plan_kernel,
        out_specs=(in_vmem,) * 3 + (in_smem,),
        out_shape=(floats(rows, width), whole_numbers(rows, width), whole_numbers(rows, width), whole_numbers(1, 1)),
        compiler_params=params,
        cost_estimate=cost,
        name="plan",
    )(sea_mask, bottom_level)

    raw = pl.pallas_call(
        pack_kernel,
        out_shape=floats(2 * SLOTS, rows // 2, width),
        compiler_params=params,
        cost_estimate=cost,
        name="pack",
    )(initial, wet, order)
    came_raw = passed_along(raw, "slab", 1)

    saved, surfaces = pl.pallas_call(
        forward_kernel,
        out_shape=(floats(SAVED, rows + 2 * HALO, width), floats(STEPS, rows + 2 * HALO, width)),
        scratch_shapes=[work(REACH)] + [pad(REACH)] * 13,
        compiler_params=params,
        cost_estimate=cost,
        name="forward",
    )(initial, above, below, water_depth, wet, drag_coef)
    came_surfaces = passed_along(surfaces, "slab", 1)

    start, gradient, start_packed = pl.pallas_call(
        adjoint_kernel,
        out_specs=(anywhere, in_vmem, in_vmem),
        out_shape=(state_shape, floats(rows, width), packed_shape),
        scratch_shapes=[work(0), pltpu.SemaphoreType.DMA(()), work(HALO)] + [pad(HALO)] * 14,
        compiler_params=params,
        cost_estimate=cost,
        name="adjoint",
    )(adjoint, misfit, saved, above, below, water_depth, wet, drag_coef, order)
    slabs = lax.axis_size("slab")
    if slabs > 4:
        gradients = [lax.psum(gradient, "slab")]
    else:
        gradients = [gradient] + [passed_along(gradient, "slab", distance) for distance in range(1, slabs)]
    start_packed, came_raw, came_surfaces = lax.optimization_barrier((start_packed, came_raw, came_surfaces))
    came_adjoint = passed_along(start_packed, "slab", -1)

    def unless_packed(sent, distance):
        return lax.cond(
            deepest[0, 0] > SLOTS,
            lambda sent: passed_along(sent, "slab", distance),
            lambda sent: pl.pallas_call(
                nothing_kernel, out_specs=anywhere, out_shape=state_shape, compiler_params=params, name="nothing"
            )(),
            sent,
        )

    next_state = pl.pallas_call(
        replay_kernel,
        in_specs=[in_smem] + [in_vmem] * 7 + [anywhere],
        out_shape=state_shape,
        scratch_shapes=[pad(0)] * 6,
        compiler_params=params,
        cost_estimate=cost,
        name="replay",
    )(deepest, came_raw, wet, order, place, water_depth, drag_coef, came_surfaces,
      unless_packed(initial, 1))

    pool = pl.BlockSpec((POOL, width), lambda i: (i, 0))
    next_adjoint, drag_total = pl.pallas_call(
        unpack_kernel,
        grid=(rows // POOL,),
        in_specs=[in_smem, pl.BlockSpec((2 * SLOTS + 2, POOL // 2, width), lambda i: (0, i, 0)),
                  pool, pool, pool, anywhere] + [pool] * len(gradients),
        out_specs=[pl.BlockSpec((fields, POOL, width), lambda i: (0, i, 0)), pool],
        out_shape=[state_shape, floats(rows, width)],
        compiler_params=params,
        cost_estimate=cost,
        name="unpack",
    )(deepest, came_adjoint, wet, order, place, unless_packed(start, -1), *gradients)
    return (next_state[None], next_adjoint[None], drag_total)


def solution(mesh):
    return jax.shard_map(
        body,
        mesh=mesh,
        in_specs=(
            P(("groups", "slab"), None, "tile", None),
            P(("groups", "slab"), None, "tile", None),
            P(("groups", "slab"), None, "tile", None),
            P(("groups", "tile"), None),
            P(("groups", "tile"), None),
            P(("groups", "tile"), None),
            P(("groups", "tile"), None),
        ),
        out_specs=(
            P(("groups", "slab"), None, "tile", None),
            P(("groups", "slab"), None, "tile", None),
            P(("groups", "tile"), None),
        ),
        check_vma=False,
    )
```

```python
import jax
import jax.numpy as jnp
from jax import lax
from jax.experimental import pallas as pl
from jax.experimental.pallas import tpu as pltpu
from jax.sharding import PartitionSpec as P

STEPS = 4
BLOCK = 8
HALO = 2 * STEPS
REACH = 2 * HALO
SAVED = 2 + 2 * STEPS
POOL = 4 * BLOCK
SLOTS = 29
LEVELS = 24


def shifted(block, axis, distance):
    devices = range(lax.axis_size(axis))
    route = [(i - distance, i) for i in devices if i - distance in devices]
    return lax.ppermute(block, axis, route)


def passed_along(block, axis, distance):
    devices = range(lax.axis_size(axis))
    route = [((i - distance) % len(devices), i) for i in devices]
    return lax.ppermute(block, axis, route)


def row_diff(values):
    return pltpu.roll(values, values.shape[0] - 1, 0) - pltpu.roll(values, 1, 0)


def column_diff(values):
    width = values.shape[1]
    lane = lax.broadcasted_iota(jnp.int32, values.shape, 1)
    after = jnp.where(lane < width - 1, pltpu.roll(values, width - 1, 1), 0.0)
    before = jnp.where(lane > 0, pltpu.roll(values, 1, 1), 0.0)
    return after - before


def looped(count, visit):
    def one(index, carry):
        visit(pl.multiple_of(index * BLOCK, BLOCK))
        return carry

    lax.fori_loop(0, count // BLOCK, one, 0)


def over_blocks(rows, halo, visit, own, above, below):
    block = lambda start: pl.ds(start if isinstance(start, int) else pl.multiple_of(start, BLOCK), BLOCK)
    looped(halo, lambda start: visit(block(start), above, block(start)))
    looped(rows, lambda start: visit(block(start + halo), own, block(start)))
    looped(halo, lambda start: visit(block(start + halo + rows), below, block(start)))


def fill_padded(target, own, above, below):
    rows, halo = own.shape[0], above.shape[0]
    target[0:halo] = above
    target[halo : halo + rows] = own
    target[halo + rows : rows + 2 * halo] = below


class Shifted:
    def __init__(self, ref, at):
        self.ref, self.at = ref, at

    def __getitem__(self, key):
        return self.ref[key[0], self.at]


class AdjointEdge:
    def __init__(self, ref, fields):
        self.ref, self.fields = ref, fields

    def __getitem__(self, key):
        plane, rows = edge_place(self.fields, key[0])
        return self.ref[plane, rows]


def edge_planes(fields):
    return fields + 3 + (fields + STEPS + 1) // 2


def edge_place(fields, item):
    first = (fields + STEPS + 1) // 2
    half = 0 if item < first else HALO
    return fields + 3 + item - (first if half else 0), pl.ds(half, HALO)


def lanes_of(values):
    return lax.broadcasted_iota(jnp.int32, values.shape, values.ndim - 1)


def take_lanes(values, index):
    return jnp.take_along_axis(values, index, axis=1, mode="promise_in_bounds")


def plan_kernel(mask, bottom, wet, order, place, deepest):
    rows, width = mask.shape
    half = width // 2
    depth = mask[...] * bottom[...]
    wet[...] = depth.astype(jnp.float32)
    lane = lanes_of(depth)
    even = (lax.broadcasted_iota(jnp.int32, depth.shape, 0) // BLOCK) % 2 == 0
    most_levels = LEVELS
    before = lax.broadcasted_iota(jnp.int32, (width, 2 * width), 0) < lax.broadcasted_iota(jnp.int32, (width, 2 * width), 1)
    same = [jnp.where(depth == level, 1.0, 0.0) for level in range(most_levels, -1, -1)]
    counts = jnp.dot(
        jnp.concatenate(same).astype(jnp.bfloat16),
        jnp.where(before, 1.0, 0.0).astype(jnp.bfloat16),
        preferred_element_type=jnp.float32,
    )
    deeper = rank = jnp.zeros(depth.shape, jnp.float32)
    for index, level in enumerate(range(most_levels, -1, -1)):
        here = counts[index * rows : (index + 1) * rows]
        rank = jnp.where(depth == level, deeper + here[:, :width], rank)
        deeper = deeper + here[:, width:]
    rank = rank.astype(jnp.int32)
    ahead = jnp.where(rank < half, rank, width + half - 1 - rank)
    behind = jnp.where(rank < half, rank + half, width - 1 - rank)
    there = jnp.where(even, ahead, behind)
    place[...] = there
    moved = jnp.zeros_like(depth)
    for shift in range(1, width):
        moved = jnp.where(pltpu.roll(there, shift, 1) == lane, shift, moved)
    origin = (lane - moved) & (width - 1)
    order[...] = origin
    most = jnp.zeros((BLOCK, width), jnp.float32)
    for pool in range(rows // POOL):
        ats = [slice(pool * POOL + block * BLOCK, pool * POOL + (block + 1) * BLOCK) for block in range(4)]
        deep, shallow, swap = pair_up([take_lanes(wet[at], origin[at]) for at in ats])
        most = jnp.maximum(most, deep[0] + jnp.where(swap, shallow[1], shallow[0]))
        most = jnp.maximum(most, deep[1] + jnp.where(swap, shallow[0], shallow[1]))
    deepest[0, 0] = jnp.max(most).astype(jnp.int32)


def deep_and_shallow(blocks):
    first = lanes_of(blocks[0]) < blocks[0].shape[1] // 2
    deep = [jnp.where(first, blocks[0], blocks[1]), jnp.where(first, blocks[2], blocks[3])]
    shallow = [jnp.where(first, blocks[1], blocks[0]), jnp.where(first, blocks[3], blocks[2])]
    return deep, shallow


def pair_up(depths):
    deep, shallow = deep_and_shallow(depths)
    swap = (deep[0] - deep[1]) * (shallow[0] - shallow[1]) > 0.0
    return deep, shallow, swap


def pool_rows(pool):
    start = pl.multiple_of(pool * POOL, POOL)
    return [pl.ds(pl.multiple_of(start + block * BLOCK, BLOCK), BLOCK) for block in range(4)]


def pool_slots(pool):
    start = pl.multiple_of(pool * (POOL // 2), POOL // 2)
    return [pl.ds(pl.multiple_of(start + block * BLOCK, BLOCK), BLOCK) for block in range(2)]


def pack(state, wet, order, packed):
    levels = (state.shape[0] - 1) // 2

    def one_pool(pool, carry):
        ats = pool_rows(pool)
        slots = pool_slots(pool)
        orders = [order[at, :] for at in ats]
        deep_wet, _, swap = pair_up([take_lanes(wet[at, :], by) for at, by in zip(ats, orders)])
        for base, target in ((1, 0), (1 + levels, SLOTS)):

            def sorted_level(level):
                parts = [take_lanes(state[base + level, at, :], by) for at, by in zip(ats, orders)]
                deep, shallow = deep_and_shallow(parts)
                return deep, (jnp.where(swap, shallow[1], shallow[0]), jnp.where(swap, shallow[0], shallow[1]))

            for near in range((SLOTS + 1) // 2):
                far = SLOTS - 1 - near
                both = far < levels
                deep, shallow = sorted_level(near)
                far_deep, far_shallow = sorted_level(far) if both and far > near else (deep, shallow)
                for half in range(2):
                    value = deep[half]
                    if both:
                        value = jnp.where(deep_wet[half] > near, value, far_shallow[half])
                    packed[target + near, slots[half], :] = value
                    if far > near:
                        value = shallow[half]
                        if both:
                            value = jnp.where(deep_wet[half] > far, far_deep[half], value)
                        packed[target + far, slots[half], :] = value
        return carry

    lax.fori_loop(0, packed.shape[1] // (POOL // 2), one_pool, 0)


def pack_kernel(state, wet, order, packed):
    pack(state, wet, order, packed)


def unpack_pool(packed, wet, order, place, state, pool):
    levels = (state.shape[0] - 1) // 2
    ats = pool_rows(pool)
    slots = pool_slots(pool)
    wets = [wet[at, :] for at in ats]
    places = [place[at, :] for at in ats]
    _, _, swap = pair_up([take_lanes(depth, order[at, :]) for depth, at in zip(wets, ats)])
    first = lanes_of(swap) < swap.shape[1] // 2
    for base, source in ((1, 0), (1 + levels, SLOTS)):

        def write_level(level, deep, ends):
            shallow = jnp.where(swap, ends[1], ends[0]), jnp.where(swap, ends[0], ends[1])
            for block in range(4):
                pair = deep[block // 2], shallow[block // 2]
                if block % 2:
                    pair = pair[::-1]
                value = take_lanes(jnp.where(first, *pair), places[block])
                state[base + level, ats[block], :] = jnp.where(wets[block] > level, value, 0.0)

        for near in range((SLOTS + 1) // 2):
            far = SLOTS - 1 - near
            head = [packed[source + near, slot, :] for slot in slots]
            tail = [packed[source + far, slot, :] for slot in slots]
            write_level(near, head, tail)
            if near < far < levels:
                write_level(far, tail, head)


def unpack_kernel(deepest, packed, wet, order, place, whole, state, done):
    done[...] = jnp.zeros_like(done)
    pool = pl.program_id(0)

    @pl.when(deepest[0, 0] > SLOTS)
    def _():
        pltpu.sync_copy(whole.at[:, pl.ds(pl.multiple_of(pool * POOL, POOL), POOL), :], state)

    @pl.when(deepest[0, 0] <= SLOTS)
    def _():
        unpack_pool(packed, wet, order, place, state, 0)
        for half in range(2):
            state[0, half * (POOL // 2) : (half + 1) * (POOL // 2)] = packed[2 * SLOTS + half]


def replay_kernel(deepest, packed, wet, order, place, depth, drag, surfaces, whole, final,
                  thick, bot_u, bot_v, slope_x, slope_y, factor):
    fields, rows, width = final.shape
    levels = (fields - 1) // 2

    @pl.when(deepest[0, 0] > SLOTS)
    def _():
        pltpu.sync_copy(whole, final)
        for level in range(levels):
            active = wet[...] > level
            for at in (1 + level, 1 + levels + level):
                final[at] = jnp.where(active, final[at], 0.0)

    @pl.when(deepest[0, 0] <= SLOTS)
    def _():
        def one_pool(pool, carry):
            unpack_pool(packed, wet, order, place, final, pool)
            return carry

        lax.fori_loop(0, rows // POOL, one_pool, 0)

    def lowest(start):
        at = pl.ds(start, BLOCK)
        wet_here = wet[at, :]
        low_u = low_v = jnp.zeros_like(wet_here)
        for level in range(levels):
            bottom = wet_here == level + 1
            low_u = jnp.where(bottom, final[1 + level, at, :], low_u)
            low_v = jnp.where(bottom, final[1 + levels + level, at, :], low_v)
        bot_u[at, :] = low_u
        bot_v[at, :] = low_v

    looped(rows, lowest)
    sea = jnp.minimum(wet[...], 1.0)
    thick[...] = depth[...] / jnp.maximum(wet[...], 1.0)
    for step in range(STEPS):
        surface = surfaces[step * rows : (step + 1) * rows]
        edges = surfaces[STEPS * rows : STEPS * rows + HALO]
        row = lax.broadcasted_iota(jnp.int32, surface.shape, 0)
        before = jnp.where(row == 0, edges[2 * step : 2 * step + 1], pltpu.roll(surface, 1, 0))
        after = jnp.where(row == rows - 1, edges[2 * step + 1 : 2 * step + 2], pltpu.roll(surface, rows - 1, 0))
        slope_x[...] = 0.2 * (after - before)
        slope_y[...] = 0.2 * column_diff(surface)
        factor[...] = drag_terms(bot_u[...], bot_v[...], thick[...], drag[...], sea)[2]

        def update(start):
            at = pl.ds(start, BLOCK)

            def store(level, u, v):
                final[1 + level, at, :] = u
                final[1 + levels + level, at, :] = v

            slow = factor[at, :]
            fetch = lambda level: (final[1 + level, at, :], final[1 + levels + level, at, :])
            _, low, _ = column_step(levels, wet[at, :], slow, slope_x[at, :], slope_y[at, :], fetch, store)
            bot_u[at, :] = slow * low[0]
            bot_v[at, :] = slow * low[1]

        looped(rows, update)
    final[0] = surfaces[(STEPS - 1) * rows : STEPS * rows]


def edge_kernel(state, adjoint, misfit, depth, drag, mask, bottom, upward, downward, sea_rows, level_rows, sems):
    fields, rows, _ = state.shape
    first = (fields + STEPS + 1) // 2
    joint = fields + 3
    copies = []

    def bring(source, target):
        copies.append(pltpu.make_async_copy(source, target, sems.at[len(copies)]))

    for side, target in enumerate((upward, downward)):
        wide = pl.ds(side * (rows - REACH), REACH)
        narrow = pl.ds(side * (rows - HALO), HALO)
        bring(state.at[:, wide, :], target.at[pl.ds(0, fields)])
        bring(adjoint.at[pl.ds(0, first), narrow, :], target.at[pl.ds(joint, first), pl.ds(0, HALO), :])
        bring(
            adjoint.at[pl.ds(first, fields - first), narrow, :],
            target.at[pl.ds(joint, fields - first), pl.ds(HALO, HALO), :],
        )
        for step in range(STEPS):
            plane, at = edge_place(fields, fields + step)
            bring(misfit.at[step, narrow, :], target.at[plane, at, :])
        bring(depth.at[wide, :], target.at[fields])
        bring(drag.at[wide, :], target.at[fields + 2])
        bring(mask.at[wide, :], sea_rows.at[side])
        bring(bottom.at[wide, :], level_rows.at[side])
    for copy in copies:
        copy.start()
    for copy in copies:
        copy.wait()
    for side, target in enumerate((upward, downward)):
        target[fields + 1] = (sea_rows[side] * level_rows[side]).astype(jnp.float32)


def total_kernel(done, *refs):
    *gradients, total = refs
    summed = gradients[0][...]
    for gradient in gradients[1:]:
        summed = summed + gradient[...]
    total[...] = summed


def nothing_kernel(result):
    pass


def drag_terms(u_bottom, v_bottom, thickness, drag, sea):
    speed = jnp.sqrt(u_bottom * u_bottom + v_bottom * v_bottom + 0.0025)
    denominator = thickness + 0.1 * drag * speed + 1.0 - sea
    return speed, denominator, thickness / denominator


def column_step(levels, wet_here, slow, grad_x, grad_y, fetch, store):
    zero = jnp.zeros_like(wet_here)
    total = low = second = (zero, zero)
    u_up = v_up = zero
    u, v = fetch(0)
    for level in range(levels):
        u_down, v_down = fetch(level + 1) if level + 1 < levels else (zero, zero)
        inside = wet_here > level + 1
        bottom = wet_here == level + 1
        above_bottom = wet_here == level + 2
        own = 1.0 if level == 0 else 0.9
        weight = jnp.where(inside, own - 0.1, own)
        retain = jnp.where(inside, 1.0, jnp.where(bottom, slow, 0.0))
        ut = weight * u + 0.1 * (v + u_up + u_down) - grad_x
        vt = weight * v + 0.1 * (v_up + v_down - u) - grad_y
        low = jnp.where(bottom, ut, low[0]), jnp.where(bottom, vt, low[1])
        u_new = ut * retain
        v_new = vt * retain
        second = jnp.where(above_bottom, u_new, second[0]), jnp.where(above_bottom, v_new, second[1])
        store(level, u_new, v_new)
        total = total[0] + u_new, total[1] + v_new
        u_up, v_up, u, v = u, v, u_down, v_down
    return total, low, second


def forward_kernel(state, above, below, depth, wet, drag, saved, surfaces,
                   work, wet_pad, thick, drag_pad, eta, sum_u, sum_v, bot_u, bot_v, next_u, next_v,
                   slope_x, slope_y, factor):
    fields, rows, _ = state.shape
    levels = (fields - 1) // 2
    kept_rows = slice(HALO, REACH + HALO + rows)
    fill_padded(wet_pad, wet[...], above[fields + 1], below[fields + 1])
    fill_padded(drag_pad, drag[...], above[fields + 2], below[fields + 2])
    fill_padded(thick, depth[...], above[fields], below[fields])
    fill_padded(eta, state[0], above[0], below[0])
    thick[...] = thick[...] / jnp.maximum(wet_pad[...], 1.0)

    def sums(at, source, source_at):
        wet_here = wet_pad[at]
        total_u = total_v = low_u = low_v = jnp.zeros_like(wet_here)
        for level in range(levels):
            active = wet_here > level
            bottom = wet_here == level + 1
            u = jnp.where(active, source[1 + level, source_at], 0.0)
            v = jnp.where(active, source[1 + levels + level, source_at], 0.0)
            total_u += u
            total_v += v
            low_u = jnp.where(bottom, u, low_u)
            low_v = jnp.where(bottom, v, low_v)
        sum_u[at] = total_u
        sum_v[at] = total_v
        bot_u[at] = low_u
        bot_v[at] = low_v

    over_blocks(rows, REACH, sums, state, above, below)
    saved[0] = bot_u[kept_rows]
    saved[1] = bot_v[kept_rows]

    for step in range(STEPS):
        sea = jnp.minimum(wet_pad[...], 1.0)
        flux_x = thick[...] * sum_u[...]
        flux_y = thick[...] * sum_v[...]
        surface = sea * (eta[...] - 0.2 * (row_diff(flux_x) + column_diff(flux_y)))
        eta[...] = surface
        surfaces[step * rows : (step + 1) * rows] = eta[REACH : REACH + rows]
        surfaces[STEPS * rows + 2 * step : STEPS * rows + 2 * step + 1] = eta[REACH - 1 : REACH]
        surfaces[STEPS * rows + 2 * step + 1 : STEPS * rows + 2 * step + 2] = eta[REACH + rows : REACH + rows + 1]
        slope_x[...] = 0.2 * row_diff(surface)
        slope_y[...] = 0.2 * column_diff(surface)
        if step == STEPS - 1:
            weight = jnp.where(wet_pad[...] > 1.0, 0.9, 1.0)
            low_u, low_v = bot_u[...], bot_v[...]
            floor = wet_pad[...] > 0.0
            last_u = weight * low_u + 0.1 * (low_v + next_u[...]) - slope_x[...]
            last_v = weight * low_v + 0.1 * (next_v[...] - low_u) - slope_y[...]
            bot_u[...] = jnp.where(floor, last_u, 0.0)
            bot_v[...] = jnp.where(floor, last_v, 0.0)
        else:
            factor[...] = drag_terms(bot_u[...], bot_v[...], thick[...], drag_pad[...], sea)[2]

            def update(at, source, source_at):
                wet_here = wet_pad[at]

                def fetch(level):
                    u = source[1 + level, source_at]
                    v = source[1 + levels + level, source_at]
                    if step == 0:
                        u = jnp.where(wet_here > level, u, 0.0)
                        v = jnp.where(wet_here > level, v, 0.0)
                    return u, v

                def store(level, u, v):
                    work[1 + level, at] = u
                    work[1 + levels + level, at] = v

                total, low, second = column_step(
                    levels, wet_here, factor[at], slope_x[at], slope_y[at], fetch, store
                )
                sum_u[at], sum_v[at] = total
                bot_u[at], bot_v[at] = low
                next_u[at], next_v[at] = second

            if step == 0:
                over_blocks(rows, REACH, update, state, above, below)
            else:
                looped(rows + 2 * REACH, lambda start: update(pl.ds(start, BLOCK), work, pl.ds(start, BLOCK)))
        saved[2 + 2 * step] = bot_u[kept_rows]
        saved[3 + 2 * step] = bot_v[kept_rows]
        if step < STEPS - 1:
            bot_u[...] = factor[...] * bot_u[...]
            bot_v[...] = factor[...] * bot_v[...]


def adjoint_kernel(adjoint, misfit, kept, above, below, depth, wet, drag, order,
                   output, gradient, packed, start, sem,
                   work, wet_pad, thick, drag_pad, eta, sum_u, sum_v, bot_u, bot_v,
                   push_x, push_y, push_low_x, push_low_y, factor, grad_pad):
    fields, rows, _ = adjoint.shape
    levels = (fields - 1) // 2
    fill_padded(wet_pad, wet[...], above[fields + 1, HALO:], below[fields + 1, :HALO])
    fill_padded(drag_pad, drag[...], above[fields + 2, HALO:], below[fields + 2, :HALO])
    fill_padded(thick, depth[...], above[fields, HALO:], below[fields, :HALO])
    above = AdjointEdge(above, fields)
    below = AdjointEdge(below, fields)
    thick[...] = thick[...] / jnp.maximum(wet_pad[...], 1.0)
    fill_padded(eta, adjoint[0], above[0, :], below[0, :])
    grad_pad[...] = jnp.zeros_like(grad_pad)
    sea = jnp.minimum(wet_pad[...], 1.0)

    before = [(kept[0], kept[1])]
    for step in range(STEPS - 1):
        slow = drag_terms(*before[step], thick[...], drag_pad[...], sea)[2]
        before.append((slow * kept[2 + 2 * step], slow * kept[3 + 2 * step]))

    def sums(at, source, source_at):
        wet_here = wet_pad[at]
        total_u = total_v = low_u = low_v = jnp.zeros_like(wet_here)
        for level in range(levels):
            active = wet_here > level
            bottom = wet_here == level + 1
            u = jnp.where(active, source[1 + level, source_at], 0.0)
            v = jnp.where(active, source[1 + levels + level, source_at], 0.0)
            total_u += u
            total_v += v
            low_u = jnp.where(bottom, u, low_u)
            low_v = jnp.where(bottom, v, low_v)
        sum_u[at] = total_u
        sum_v[at] = total_v
        bot_u[at] = low_u
        bot_v[at] = low_v

    over_blocks(rows, HALO, sums, adjoint, above, below)

    for step in reversed(range(STEPS)):
        first, last = step == STEPS - 1, step == 0
        sea = jnp.minimum(wet_pad[...], 1.0)
        fill_padded(push_x, misfit[step], above[fields + step, :], below[fields + step, :])
        u_before, v_before = before[step]
        speed, denominator, slow = drag_terms(u_before, v_before, thick[...], drag_pad[...], sea)
        factor[...] = slow
        low_u, low_v = bot_u[...], bot_v[...]
        on_factor = low_u * kept[2 + 2 * step] + low_v * kept[3 + 2 * step]
        on_denominator = -on_factor * slow / denominator
        grad_pad[...] += 0.1 * speed * on_denominator
        on_speed = 0.1 * drag_pad[...] * on_denominator / speed
        loss = 1.0 - slow
        total_x = sum_u[...] - loss * low_u
        total_y = sum_v[...] - loss * low_v
        surface = sea * (eta[...] + push_x[...] + 0.2 * (row_diff(total_x) + column_diff(total_y)))
        eta[...] = surface
        thin = 0.2 * thick[...]
        toward_x = thin * row_diff(surface)
        toward_y = thin * column_diff(surface)
        push_x[...] = toward_x
        push_y[...] = toward_y
        push_low_x[...] = toward_x + on_speed * u_before
        push_low_y[...] = toward_y + on_speed * v_before

        def update(at, source, source_at, offset=0):
            if offset:
                at = source.at
            wet_here = wet_pad[at]
            slow_here = factor[at]
            along_x, along_y = push_x[at], push_y[at]
            low_x, low_y = push_low_x[at], push_low_y[at]
            zero = jnp.zeros_like(wet_here)
            total_u = total_v = low_u = low_v = zero

            def fetch(level):
                if level == levels:
                    return zero, zero
                retain = jnp.where(wet_here > level + 1, 1.0, jnp.where(wet_here > level, slow_here, 0.0))
                return retain * source[1 + level, source_at], retain * source[1 + levels + level, source_at]

            p_up = q_up = zero
            p, q = fetch(0)
            for level in range(levels):
                p_down, q_down = fetch(level + 1)
                inside = wet_here > level + 1
                bottom = wet_here == level + 1
                active = wet_here > level
                own = 1.0 if level == 0 else 0.9
                weight = jnp.where(inside, own - 0.1, own)
                u = weight * p + 0.1 * (p_up + p_down - q) + jnp.where(inside, along_x, low_x)
                v = weight * q + 0.1 * (q_up + q_down + p) + jnp.where(inside, along_y, low_y)
                u = jnp.where(active, u, 0.0)
                v = jnp.where(active, v, 0.0)
                if last:
                    start[1 + level, source_at] = u
                    start[1 + levels + level, source_at] = v
                else:
                    work[1 + level, at] = u
                    work[1 + levels + level, at] = v
                    total_u += u
                    total_v += v
                    low_u = jnp.where(bottom, u, low_u)
                    low_v = jnp.where(bottom, v, low_v)
                p_up, q_up, p, q = p, q, p_down, q_down
            if not last:
                sum_u[at] = total_u
                sum_v[at] = total_v
                bot_u[at] = low_u
                bot_v[at] = low_v

        if first:
            over_blocks(rows, HALO, update, adjoint, above, below)
        elif last:

            def into_start(begin):
                update(pl.ds(begin, BLOCK), Shifted(work, pl.ds(pl.multiple_of(begin + HALO, BLOCK), BLOCK)),
                       pl.ds(begin, BLOCK), HALO)

            looped(rows, into_start)
        else:

            def in_place(begin):
                at = pl.ds(begin, BLOCK)
                update(at, work, at)

            looped(rows + 2 * HALO, in_place)
    start[0] = eta[HALO : HALO + rows]
    gradient[...] = grad_pad[HALO : HALO + rows]
    copy = pltpu.make_async_copy(start, output, sem)
    copy.start()
    pack(start, wet, order, packed)
    for pool in range(rows // POOL):
        for half in range(2):
            at = pool * POOL + half * (POOL // 2)
            packed[2 * SLOTS + half, pool * (POOL // 2) : (pool + 1) * (POOL // 2)] = start[0, at : at + POOL // 2]
    copy.wait()


def body(start_states, end_adjoints, misfits, water_depth, drag_coef, sea_mask, bottom_level):
    initial = start_states[0]
    adjoint = end_adjoints[0]
    misfit = misfits[0]
    fields, rows, width = initial.shape
    floats = lambda *shape: jax.ShapeDtypeStruct(shape, jnp.float32)
    whole_numbers = lambda *shape: jax.ShapeDtypeStruct(shape, jnp.int32)
    pad = lambda halo: pltpu.VMEM((rows + 2 * halo, width), jnp.float32)
    work = lambda halo: pltpu.VMEM((fields, rows + 2 * halo, width), jnp.float32)
    params = pltpu.CompilerParams(vmem_limit_bytes=16 << 20)
    cells = fields * rows * width
    cost = pl.CostEstimate(flops=100 * cells, bytes_accessed=10 * cells, transcendentals=0)
    state_shape = floats(fields, rows, width)
    packed_shape = floats(2 * SLOTS + 2, rows // 2, width)
    edge_shape = floats(edge_planes(fields), REACH, width)
    in_vmem = pl.BlockSpec(memory_space=pltpu.VMEM)
    in_smem = pl.BlockSpec(memory_space=pltpu.SMEM)
    anywhere = pl.BlockSpec(memory_space=pl.ANY)

    upward, downward = pl.pallas_call(
        edge_kernel,
        in_specs=[anywhere] * 7,
        out_specs=(in_vmem, in_vmem),
        out_shape=(edge_shape, edge_shape),
        scratch_shapes=[pltpu.VMEM((2, REACH, width), jnp.int32)] * 2 + [pltpu.SemaphoreType.DMA((22,))],
        compiler_params=params,
        cost_estimate=cost,
        name="edges",
    )(initial, adjoint, misfit, water_depth, drag_coef, sea_mask, bottom_level)
    above = shifted(downward, "tile", 1)
    below = shifted(upward, "tile", -1)

    wet, order, place, deepest = pl.pallas_call(
        plan_kernel,
        out_specs=(in_vmem,) * 3 + (in_smem,),
        out_shape=(floats(rows, width), whole_numbers(rows, width), whole_numbers(rows, width), whole_numbers(1, 1)),
        compiler_params=params,
        cost_estimate=cost,
        name="plan",
    )(sea_mask, bottom_level)

    raw = pl.pallas_call(
        pack_kernel,
        out_shape=floats(2 * SLOTS, rows // 2, width),
        compiler_params=params,
        cost_estimate=cost,
        name="pack",
    )(initial, wet, order)
    came_raw = passed_along(raw, "slab", 1)

    saved, surfaces = pl.pallas_call(
        forward_kernel,
        out_shape=(floats(SAVED, rows + 2 * HALO, width), floats(STEPS * rows + HALO, width)),
        scratch_shapes=[work(REACH)] + [pad(REACH)] * 13,
        compiler_params=params,
        cost_estimate=cost,
        name="forward",
    )(initial, above, below, water_depth, wet, drag_coef)
    came_surfaces = passed_along(surfaces, "slab", 1)

    start, gradient, start_packed = pl.pallas_call(
        adjoint_kernel,
        out_specs=(anywhere, in_vmem, in_vmem),
        out_shape=(state_shape, floats(rows, width), packed_shape),
        scratch_shapes=[work(0), pltpu.SemaphoreType.DMA(()), work(HALO)] + [pad(HALO)] * 14,
        compiler_params=params,
        cost_estimate=cost,
        name="adjoint",
    )(adjoint, misfit, saved, above, below, water_depth, wet, drag_coef, order)
    slabs = lax.axis_size("slab")
    if slabs > 4:
        gradients = [lax.psum(gradient, "slab")]
    else:
        gradients = [gradient] + [passed_along(gradient, "slab", distance) for distance in range(1, slabs)]
    start_packed, came_raw, came_surfaces = lax.optimization_barrier((start_packed, came_raw, came_surfaces))
    came_adjoint = passed_along(start_packed, "slab", -1)

    def unless_packed(sent, distance):
        return lax.cond(
            deepest[0, 0] > SLOTS,
            lambda sent: passed_along(sent, "slab", distance),
            lambda sent: pl.pallas_call(
                nothing_kernel, out_specs=anywhere, out_shape=state_shape, compiler_params=params, name="nothing"
            )(),
            sent,
        )

    next_state = pl.pallas_call(
        replay_kernel,
        in_specs=[in_smem] + [in_vmem] * 7 + [anywhere],
        out_shape=state_shape,
        scratch_shapes=[pad(0)] * 6,
        compiler_params=params,
        cost_estimate=cost,
        name="replay",
    )(deepest, came_raw, wet, order, place, water_depth, drag_coef, came_surfaces,
      unless_packed(initial, 1))

    pool = pl.BlockSpec((POOL, width), lambda i: (i, 0))
    next_adjoint, done = pl.pallas_call(
        unpack_kernel,
        grid=(rows // POOL,),
        in_specs=[in_smem, pl.BlockSpec((2 * SLOTS + 2, POOL // 2, width), lambda i: (0, i, 0)),
                  pool, pool, pool, anywhere],
        out_specs=[pl.BlockSpec((fields, POOL, width), lambda i: (0, i, 0)),
                   pl.BlockSpec((BLOCK, width), lambda i: (0, 0))],
        out_shape=[state_shape, floats(BLOCK, width)],
        compiler_params=params,
        cost_estimate=cost,
        name="unpack",
    )(deepest, came_adjoint, wet, order, place, unless_packed(start, -1))
    drag_total = pl.pallas_call(
        total_kernel, out_shape=floats(rows, width), compiler_params=params, cost_estimate=cost, name="total"
    )(done, *gradients)
    return (next_state[None], next_adjoint[None], drag_total)


def solution(mesh):
    return jax.shard_map(
        body,
        mesh=mesh,
        in_specs=(
            P(("groups", "slab"), None, "tile", None),
            P(("groups", "slab"), None, "tile", None),
            P(("groups", "slab"), None, "tile", None),
            P(("groups", "tile"), None),
            P(("groups", "tile"), None),
            P(("groups", "tile"), None),
            P(("groups", "tile"), None),
        ),
        out_specs=(
            P(("groups", "slab"), None, "tile", None),
            P(("groups", "slab"), None, "tile", None),
            P(("groups", "tile"), None),
        ),
        check_vma=False,
    )
```

```python
import jax
import jax.numpy as jnp
from jax import lax
from jax.experimental import pallas as pl
from jax.experimental.pallas import tpu as pltpu
from jax.sharding import PartitionSpec as P

STEPS = 4
BLOCK = 8
HALO = 2 * STEPS
REACH = 2 * HALO
SAVED = 2 + 2 * STEPS
POOL = 4 * BLOCK
SLOTS = 29
LEVELS = 24


def shifted(block, axis, distance):
    devices = range(lax.axis_size(axis))
    route = [(i - distance, i) for i in devices if i - distance in devices]
    return lax.ppermute(block, axis, route)


def passed_along(block, axis, distance):
    devices = range(lax.axis_size(axis))
    route = [((i - distance) % len(devices), i) for i in devices]
    return lax.ppermute(block, axis, route)


def row_diff(values):
    return pltpu.roll(values, values.shape[0] - 1, 0) - pltpu.roll(values, 1, 0)


def column_diff(values):
    width = values.shape[1]
    lane = lax.broadcasted_iota(jnp.int32, values.shape, 1)
    after = jnp.where(lane < width - 1, pltpu.roll(values, width - 1, 1), 0.0)
    before = jnp.where(lane > 0, pltpu.roll(values, 1, 1), 0.0)
    return after - before


def looped(count, visit):
    def one(index, carry):
        visit(pl.multiple_of(index * BLOCK, BLOCK))
        return carry

    lax.fori_loop(0, count // BLOCK, one, 0)


def over_blocks(rows, halo, visit, own, above, below):
    block = lambda start: pl.ds(start if isinstance(start, int) else pl.multiple_of(start, BLOCK), BLOCK)
    looped(halo, lambda start: visit(block(start), above, block(start)))
    looped(rows, lambda start: visit(block(start + halo), own, block(start)))
    looped(halo, lambda start: visit(block(start + halo + rows), below, block(start)))


def fill_padded(target, own, above, below):
    rows, halo = own.shape[0], above.shape[0]
    target[0:halo] = above
    target[halo : halo + rows] = own
    target[halo + rows : rows + 2 * halo] = below


class Shifted:
    def __init__(self, ref, at):
        self.ref, self.at = ref, at

    def __getitem__(self, key):
        return self.ref[key[0], self.at]


class AdjointEdge:
    def __init__(self, ref, fields):
        self.ref, self.fields = ref, fields

    def __getitem__(self, key):
        plane, rows = edge_place(self.fields, key[0])
        return self.ref[plane, rows]


def edge_planes(fields):
    return fields + 3 + (fields + STEPS + 1) // 2


def edge_place(fields, item):
    first = (fields + STEPS + 1) // 2
    half = 0 if item < first else HALO
    return fields + 3 + item - (first if half else 0), pl.ds(half, HALO)


def lanes_of(values):
    return lax.broadcasted_iota(jnp.int32, values.shape, values.ndim - 1)


def take_lanes(values, index):
    return jnp.take_along_axis(values, index, axis=1, mode="promise_in_bounds")


def plan_kernel(wet_levels, wet, order, place, deepest):
    rows, width = wet_levels.shape
    half = width // 2
    depth = wet_levels[...]
    wet[...] = depth.astype(jnp.float32)
    lane = lanes_of(depth)
    even = (lax.broadcasted_iota(jnp.int32, depth.shape, 0) // BLOCK) % 2 == 0
    most_levels = LEVELS
    before = lax.broadcasted_iota(jnp.int32, (width, 2 * width), 0) < lax.broadcasted_iota(jnp.int32, (width, 2 * width), 1)
    same = [jnp.where(depth == level, 1.0, 0.0) for level in range(most_levels, -1, -1)]
    counts = jnp.dot(
        jnp.concatenate(same).astype(jnp.bfloat16),
        jnp.where(before, 1.0, 0.0).astype(jnp.bfloat16),
        preferred_element_type=jnp.float32,
    )
    deeper = rank = jnp.zeros(depth.shape, jnp.float32)
    for index, level in enumerate(range(most_levels, -1, -1)):
        here = counts[index * rows : (index + 1) * rows]
        rank = jnp.where(depth == level, deeper + here[:, :width], rank)
        deeper = deeper + here[:, width:]
    rank = rank.astype(jnp.int32)
    ahead = jnp.where(rank < half, rank, width + half - 1 - rank)
    behind = jnp.where(rank < half, rank + half, width - 1 - rank)
    there = jnp.where(even, ahead, behind)
    place[...] = there
    moved = jnp.zeros_like(depth)
    for shift in range(1, width):
        moved = jnp.where(pltpu.roll(there, shift, 1) == lane, shift, moved)
    origin = (lane - moved) & (width - 1)
    order[...] = origin
    most = jnp.zeros((BLOCK, width), jnp.float32)
    for pool in range(rows // POOL):
        ats = [slice(pool * POOL + block * BLOCK, pool * POOL + (block + 1) * BLOCK) for block in range(4)]
        deep, shallow, swap = pair_up([take_lanes(wet[at], origin[at]) for at in ats])
        most = jnp.maximum(most, deep[0] + jnp.where(swap, shallow[1], shallow[0]))
        most = jnp.maximum(most, deep[1] + jnp.where(swap, shallow[0], shallow[1]))
    deepest[0, 0] = jnp.max(most).astype(jnp.int32)


def deep_and_shallow(blocks):
    first = lanes_of(blocks[0]) < blocks[0].shape[1] // 2
    deep = [jnp.where(first, blocks[0], blocks[1]), jnp.where(first, blocks[2], blocks[3])]
    shallow = [jnp.where(first, blocks[1], blocks[0]), jnp.where(first, blocks[3], blocks[2])]
    return deep, shallow


def pair_up(depths):
    deep, shallow = deep_and_shallow(depths)
    swap = (deep[0] - deep[1]) * (shallow[0] - shallow[1]) > 0.0
    return deep, shallow, swap


def pool_rows(pool):
    start = pl.multiple_of(pool * POOL, POOL)
    return [pl.ds(pl.multiple_of(start + block * BLOCK, BLOCK), BLOCK) for block in range(4)]


def pool_slots(pool):
    start = pl.multiple_of(pool * (POOL // 2), POOL // 2)
    return [pl.ds(pl.multiple_of(start + block * BLOCK, BLOCK), BLOCK) for block in range(2)]


def pack(state, wet, order, packed):
    levels = (state.shape[0] - 1) // 2

    def one_pool(pool, carry):
        ats = pool_rows(pool)
        slots = pool_slots(pool)
        orders = [order[at, :] for at in ats]
        deep_wet, _, swap = pair_up([take_lanes(wet[at, :], by) for at, by in zip(ats, orders)])
        for base, target in ((1, 0), (1 + levels, SLOTS)):

            def sorted_level(level):
                parts = [take_lanes(state[base + level, at, :], by) for at, by in zip(ats, orders)]
                deep, shallow = deep_and_shallow(parts)
                return deep, (jnp.where(swap, shallow[1], shallow[0]), jnp.where(swap, shallow[0], shallow[1]))

            for near in range((SLOTS + 1) // 2):
                far = SLOTS - 1 - near
                both = far < levels
                deep, shallow = sorted_level(near)
                far_deep, far_shallow = sorted_level(far) if both and far > near else (deep, shallow)
                for half in range(2):
                    value = deep[half]
                    if both:
                        value = jnp.where(deep_wet[half] > near, value, far_shallow[half])
                    packed[target + near, slots[half], :] = value
                    if far > near:
                        value = shallow[half]
                        if both:
                            value = jnp.where(deep_wet[half] > far, far_deep[half], value)
                        packed[target + far, slots[half], :] = value
        return carry

    lax.fori_loop(0, packed.shape[1] // (POOL // 2), one_pool, 0)


def pack_kernel(state, wet, order, packed):
    pack(state, wet, order, packed)


def unpack_pool(packed, wet, order, place, state, pool):
    levels = (state.shape[0] - 1) // 2
    ats = pool_rows(pool)
    slots = pool_slots(pool)
    wets = [wet[at, :] for at in ats]
    places = [place[at, :] for at in ats]
    _, _, swap = pair_up([take_lanes(depth, order[at, :]) for depth, at in zip(wets, ats)])
    first = lanes_of(swap) < swap.shape[1] // 2
    for base, source in ((1, 0), (1 + levels, SLOTS)):

        def write_level(level, deep, ends):
            shallow = jnp.where(swap, ends[1], ends[0]), jnp.where(swap, ends[0], ends[1])
            for block in range(4):
                pair = deep[block // 2], shallow[block // 2]
                if block % 2:
                    pair = pair[::-1]
                value = take_lanes(jnp.where(first, *pair), places[block])
                state[base + level, ats[block], :] = jnp.where(wets[block] > level, value, 0.0)

        for near in range((SLOTS + 1) // 2):
            far = SLOTS - 1 - near
            head = [packed[source + near, slot, :] for slot in slots]
            tail = [packed[source + far, slot, :] for slot in slots]
            write_level(near, head, tail)
            if near < far < levels:
                write_level(far, tail, head)


def unpack_kernel(deepest, packed, wet, order, place, whole, state, done):
    done[...] = jnp.zeros_like(done)
    pool = pl.program_id(0)

    @pl.when(deepest[0, 0] > SLOTS)
    def _():
        pltpu.sync_copy(whole.at[:, pl.ds(pl.multiple_of(pool * POOL, POOL), POOL), :], state)

    @pl.when(deepest[0, 0] <= SLOTS)
    def _():
        unpack_pool(packed, wet, order, place, state, 0)
        for half in range(2):
            state[0, half * (POOL // 2) : (half + 1) * (POOL // 2)] = packed[2 * SLOTS + half]


def replay_kernel(deepest, packed, wet, order, place, depth, drag, surfaces, whole, final,
                  thick, bot_u, bot_v, slope_x, slope_y, factor):
    fields, rows, width = final.shape
    levels = (fields - 1) // 2

    @pl.when(deepest[0, 0] > SLOTS)
    def _():
        pltpu.sync_copy(whole, final)
        for level in range(levels):
            active = wet[...] > level
            for at in (1 + level, 1 + levels + level):
                final[at] = jnp.where(active, final[at], 0.0)

    @pl.when(deepest[0, 0] <= SLOTS)
    def _():
        def one_pool(pool, carry):
            unpack_pool(packed, wet, order, place, final, pool)
            return carry

        lax.fori_loop(0, rows // POOL, one_pool, 0)

    def lowest(start):
        at = pl.ds(start, BLOCK)
        wet_here = wet[at, :]
        low_u = low_v = jnp.zeros_like(wet_here)
        for level in range(levels):
            bottom = wet_here == level + 1
            low_u = jnp.where(bottom, final[1 + level, at, :], low_u)
            low_v = jnp.where(bottom, final[1 + levels + level, at, :], low_v)
        bot_u[at, :] = low_u
        bot_v[at, :] = low_v

    looped(rows, lowest)
    sea = jnp.minimum(wet[...], 1.0)
    thick[...] = depth[...] / jnp.maximum(wet[...], 1.0)
    for step in range(STEPS):
        surface = surfaces[step * rows : (step + 1) * rows]
        edges = surfaces[STEPS * rows : STEPS * rows + HALO]
        row = lax.broadcasted_iota(jnp.int32, surface.shape, 0)
        before = jnp.where(row == 0, edges[2 * step : 2 * step + 1], pltpu.roll(surface, 1, 0))
        after = jnp.where(row == rows - 1, edges[2 * step + 1 : 2 * step + 2], pltpu.roll(surface, rows - 1, 0))
        slope_x[...] = 0.2 * (after - before)
        slope_y[...] = 0.2 * column_diff(surface)
        factor[...] = drag_terms(bot_u[...], bot_v[...], thick[...], drag[...], sea)[2]

        def update(start):
            at = pl.ds(start, BLOCK)

            def store(level, u, v):
                final[1 + level, at, :] = u
                final[1 + levels + level, at, :] = v

            slow = factor[at, :]
            fetch = lambda level: (final[1 + level, at, :], final[1 + levels + level, at, :])
            _, low, _ = column_step(levels, wet[at, :], slow, slope_x[at, :], slope_y[at, :], fetch, store)
            bot_u[at, :] = slow * low[0]
            bot_v[at, :] = slow * low[1]

        looped(rows, update)
    final[0] = surfaces[(STEPS - 1) * rows : STEPS * rows]


def edge_kernel(state, adjoint, misfit, depth, drag, wet_levels, upward, downward, level_rows, sems):
    fields, rows, _ = state.shape
    first = (fields + STEPS + 1) // 2
    joint = fields + 3
    copies = []

    def bring(source, target):
        copies.append(pltpu.make_async_copy(source, target, sems.at[len(copies)]))

    for side, target in enumerate((upward, downward)):
        wide = pl.ds(side * (rows - REACH), REACH)
        narrow = pl.ds(side * (rows - HALO), HALO)
        bring(state.at[:, wide, :], target.at[pl.ds(0, fields)])
        bring(adjoint.at[pl.ds(0, first), narrow, :], target.at[pl.ds(joint, first), pl.ds(0, HALO), :])
        bring(
            adjoint.at[pl.ds(first, fields - first), narrow, :],
            target.at[pl.ds(joint, fields - first), pl.ds(HALO, HALO), :],
        )
        for step in range(STEPS):
            plane, at = edge_place(fields, fields + step)
            bring(misfit.at[step, narrow, :], target.at[plane, at, :])
        bring(depth.at[wide, :], target.at[fields])
        bring(drag.at[wide, :], target.at[fields + 2])
        bring(wet_levels.at[wide, :], level_rows.at[side])
    for copy in copies:
        copy.start()
    for copy in copies:
        copy.wait()
    for side, target in enumerate((upward, downward)):
        target[fields + 1] = level_rows[side].astype(jnp.float32)


def total_kernel(done, *refs):
    *gradients, total = refs
    summed = gradients[0][...]
    for gradient in gradients[1:]:
        summed = summed + gradient[...]
    total[...] = summed


def nothing_kernel(result):
    pass


def drag_terms(u_bottom, v_bottom, thickness, drag, sea):
    speed = jnp.sqrt(u_bottom * u_bottom + v_bottom * v_bottom + 0.0025)
    denominator = thickness + 0.1 * drag * speed + 1.0 - sea
    return speed, denominator, thickness / denominator


def column_step(levels, wet_here, slow, grad_x, grad_y, fetch, store):
    zero = jnp.zeros_like(wet_here)
    total = low = second = (zero, zero)
    u_up = v_up = zero
    u, v = fetch(0)
    for level in range(levels):
        u_down, v_down = fetch(level + 1) if level + 1 < levels else (zero, zero)
        inside = wet_here > level + 1
        bottom = wet_here == level + 1
        above_bottom = wet_here == level + 2
        own = 1.0 if level == 0 else 0.9
        weight = jnp.where(inside, own - 0.1, own)
        retain = jnp.where(inside, 1.0, jnp.where(bottom, slow, 0.0))
        ut = weight * u + 0.1 * (v + u_up + u_down) - grad_x
        vt = weight * v + 0.1 * (v_up + v_down - u) - grad_y
        low = jnp.where(bottom, ut, low[0]), jnp.where(bottom, vt, low[1])
        u_new = ut * retain
        v_new = vt * retain
        second = jnp.where(above_bottom, u_new, second[0]), jnp.where(above_bottom, v_new, second[1])
        store(level, u_new, v_new)
        total = total[0] + u_new, total[1] + v_new
        u_up, v_up, u, v = u, v, u_down, v_down
    return total, low, second


def forward_kernel(state, above, below, depth, wet, drag, saved, surfaces,
                   work, wet_pad, thick, drag_pad, eta, sum_u, sum_v, bot_u, bot_v, next_u, next_v,
                   slope_x, slope_y, factor):
    fields, rows, _ = state.shape
    levels = (fields - 1) // 2
    kept_rows = slice(HALO, REACH + HALO + rows)
    fill_padded(wet_pad, wet[...], above[fields + 1], below[fields + 1])
    fill_padded(drag_pad, drag[...], above[fields + 2], below[fields + 2])
    fill_padded(thick, depth[...], above[fields], below[fields])
    fill_padded(eta, state[0], above[0], below[0])
    thick[...] = thick[...] / jnp.maximum(wet_pad[...], 1.0)

    def sums(at, source, source_at):
        wet_here = wet_pad[at]
        total_u = total_v = low_u = low_v = jnp.zeros_like(wet_here)
        for level in range(levels):
            active = wet_here > level
            bottom = wet_here == level + 1
            u = jnp.where(active, source[1 + level, source_at], 0.0)
            v = jnp.where(active, source[1 + levels + level, source_at], 0.0)
            total_u += u
            total_v += v
            low_u = jnp.where(bottom, u, low_u)
            low_v = jnp.where(bottom, v, low_v)
        sum_u[at] = total_u
        sum_v[at] = total_v
        bot_u[at] = low_u
        bot_v[at] = low_v

    over_blocks(rows, REACH, sums, state, above, below)
    saved[0] = bot_u[kept_rows]
    saved[1] = bot_v[kept_rows]

    for step in range(STEPS):
        sea = jnp.minimum(wet_pad[...], 1.0)
        flux_x = thick[...] * sum_u[...]
        flux_y = thick[...] * sum_v[...]
        surface = sea * (eta[...] - 0.2 * (row_diff(flux_x) + column_diff(flux_y)))
        eta[...] = surface
        surfaces[step * rows : (step + 1) * rows] = eta[REACH : REACH + rows]
        surfaces[STEPS * rows + 2 * step : STEPS * rows + 2 * step + 1] = eta[REACH - 1 : REACH]
        surfaces[STEPS * rows + 2 * step + 1 : STEPS * rows + 2 * step + 2] = eta[REACH + rows : REACH + rows + 1]
        slope_x[...] = 0.2 * row_diff(surface)
        slope_y[...] = 0.2 * column_diff(surface)
        if step == STEPS - 1:
            weight = jnp.where(wet_pad[...] > 1.0, 0.9, 1.0)
            low_u, low_v = bot_u[...], bot_v[...]
            floor = wet_pad[...] > 0.0
            last_u = weight * low_u + 0.1 * (low_v + next_u[...]) - slope_x[...]
            last_v = weight * low_v + 0.1 * (next_v[...] - low_u) - slope_y[...]
            bot_u[...] = jnp.where(floor, last_u, 0.0)
            bot_v[...] = jnp.where(floor, last_v, 0.0)
        else:
            factor[...] = drag_terms(bot_u[...], bot_v[...], thick[...], drag_pad[...], sea)[2]

            def update(at, source, source_at):
                wet_here = wet_pad[at]

                def fetch(level):
                    u = source[1 + level, source_at]
                    v = source[1 + levels + level, source_at]
                    if step == 0:
                        u = jnp.where(wet_here > level, u, 0.0)
                        v = jnp.where(wet_here > level, v, 0.0)
                    return u, v

                def store(level, u, v):
                    work[1 + level, at] = u
                    work[1 + levels + level, at] = v

                total, low, second = column_step(
                    levels, wet_here, factor[at], slope_x[at], slope_y[at], fetch, store
                )
                sum_u[at], sum_v[at] = total
                bot_u[at], bot_v[at] = low
                next_u[at], next_v[at] = second

            if step == 0:
                over_blocks(rows, REACH, update, state, above, below)
            else:
                looped(rows + 2 * REACH, lambda start: update(pl.ds(start, BLOCK), work, pl.ds(start, BLOCK)))
        saved[2 + 2 * step] = bot_u[kept_rows]
        saved[3 + 2 * step] = bot_v[kept_rows]
        if step < STEPS - 1:
            bot_u[...] = factor[...] * bot_u[...]
            bot_v[...] = factor[...] * bot_v[...]


def adjoint_kernel(adjoint, misfit, kept, above, below, depth, wet, drag, order,
                   output, gradient, packed, start, sem,
                   work, wet_pad, thick, drag_pad, eta, sum_u, sum_v, bot_u, bot_v,
                   push_x, push_y, push_low_x, push_low_y, factor, grad_pad):
    fields, rows, _ = adjoint.shape
    levels = (fields - 1) // 2
    fill_padded(wet_pad, wet[...], above[fields + 1, HALO:], below[fields + 1, :HALO])
    fill_padded(drag_pad, drag[...], above[fields + 2, HALO:], below[fields + 2, :HALO])
    fill_padded(thick, depth[...], above[fields, HALO:], below[fields, :HALO])
    above = AdjointEdge(above, fields)
    below = AdjointEdge(below, fields)
    thick[...] = thick[...] / jnp.maximum(wet_pad[...], 1.0)
    fill_padded(eta, adjoint[0], above[0, :], below[0, :])
    grad_pad[...] = jnp.zeros_like(grad_pad)
    sea = jnp.minimum(wet_pad[...], 1.0)

    before = [(kept[0], kept[1])]
    for step in range(STEPS - 1):
        slow = drag_terms(*before[step], thick[...], drag_pad[...], sea)[2]
        before.append((slow * kept[2 + 2 * step], slow * kept[3 + 2 * step]))

    def sums(at, source, source_at):
        wet_here = wet_pad[at]
        total_u = total_v = low_u = low_v = jnp.zeros_like(wet_here)
        for level in range(levels):
            active = wet_here > level
            bottom = wet_here == level + 1
            u = jnp.where(active, source[1 + level, source_at], 0.0)
            v = jnp.where(active, source[1 + levels + level, source_at], 0.0)
            total_u += u
            total_v += v
            low_u = jnp.where(bottom, u, low_u)
            low_v = jnp.where(bottom, v, low_v)
        sum_u[at] = total_u
        sum_v[at] = total_v
        bot_u[at] = low_u
        bot_v[at] = low_v

    over_blocks(rows, HALO, sums, adjoint, above, below)

    for step in reversed(range(STEPS)):
        first, last = step == STEPS - 1, step == 0
        sea = jnp.minimum(wet_pad[...], 1.0)
        fill_padded(push_x, misfit[step], above[fields + step, :], below[fields + step, :])
        u_before, v_before = before[step]
        speed, denominator, slow = drag_terms(u_before, v_before, thick[...], drag_pad[...], sea)
        factor[...] = slow
        low_u, low_v = bot_u[...], bot_v[...]
        on_factor = low_u * kept[2 + 2 * step] + low_v * kept[3 + 2 * step]
        on_denominator = -on_factor * slow / denominator
        grad_pad[...] += 0.1 * speed * on_denominator
        on_speed = 0.1 * drag_pad[...] * on_denominator / speed
        loss = 1.0 - slow
        total_x = sum_u[...] - loss * low_u
        total_y = sum_v[...] - loss * low_v
        surface = sea * (eta[...] + push_x[...] + 0.2 * (row_diff(total_x) + column_diff(total_y)))
        eta[...] = surface
        thin = 0.2 * thick[...]
        toward_x = thin * row_diff(surface)
        toward_y = thin * column_diff(surface)
        push_x[...] = toward_x
        push_y[...] = toward_y
        push_low_x[...] = toward_x + on_speed * u_before
        push_low_y[...] = toward_y + on_speed * v_before

        def update(at, source, source_at, offset=0):
            if offset:
                at = source.at
            wet_here = wet_pad[at]
            slow_here = factor[at]
            along_x, along_y = push_x[at], push_y[at]
            low_x, low_y = push_low_x[at], push_low_y[at]
            zero = jnp.zeros_like(wet_here)
            total_u = total_v = low_u = low_v = zero

            def fetch(level):
                if level == levels:
                    return zero, zero
                retain = jnp.where(wet_here > level + 1, 1.0, jnp.where(wet_here > level, slow_here, 0.0))
                return retain * source[1 + level, source_at], retain * source[1 + levels + level, source_at]

            p_up = q_up = zero
            p, q = fetch(0)
            for level in range(levels):
                p_down, q_down = fetch(level + 1)
                inside = wet_here > level + 1
                bottom = wet_here == level + 1
                active = wet_here > level
                own = 1.0 if level == 0 else 0.9
                weight = jnp.where(inside, own - 0.1, own)
                u = weight * p + 0.1 * (p_up + p_down - q) + jnp.where(inside, along_x, low_x)
                v = weight * q + 0.1 * (q_up + q_down + p) + jnp.where(inside, along_y, low_y)
                u = jnp.where(active, u, 0.0)
                v = jnp.where(active, v, 0.0)
                if last:
                    start[1 + level, source_at] = u
                    start[1 + levels + level, source_at] = v
                else:
                    work[1 + level, at] = u
                    work[1 + levels + level, at] = v
                    total_u += u
                    total_v += v
                    low_u = jnp.where(bottom, u, low_u)
                    low_v = jnp.where(bottom, v, low_v)
                p_up, q_up, p, q = p, q, p_down, q_down
            if not last:
                sum_u[at] = total_u
                sum_v[at] = total_v
                bot_u[at] = low_u
                bot_v[at] = low_v

        if first:
            over_blocks(rows, HALO, update, adjoint, above, below)
        elif last:

            def into_start(begin):
                update(pl.ds(begin, BLOCK), Shifted(work, pl.ds(pl.multiple_of(begin + HALO, BLOCK), BLOCK)),
                       pl.ds(begin, BLOCK), HALO)

            looped(rows, into_start)
        else:

            def in_place(begin):
                at = pl.ds(begin, BLOCK)
                update(at, work, at)

            looped(rows + 2 * HALO, in_place)
    start[0] = eta[HALO : HALO + rows]
    gradient[...] = grad_pad[HALO : HALO + rows]
    copy = pltpu.make_async_copy(start, output, sem)
    copy.start()
    pack(start, wet, order, packed)
    for pool in range(rows // POOL):
        for half in range(2):
            at = pool * POOL + half * (POOL // 2)
            packed[2 * SLOTS + half, pool * (POOL // 2) : (pool + 1) * (POOL // 2)] = start[0, at : at + POOL // 2]
    copy.wait()


def body(start_states, end_adjoints, misfits, water_depth, drag_coef, sea_mask, bottom_level):
    initial = start_states[0]
    adjoint = end_adjoints[0]
    misfit = misfits[0]
    wet_levels = sea_mask * bottom_level
    fields, rows, width = initial.shape
    floats = lambda *shape: jax.ShapeDtypeStruct(shape, jnp.float32)
    whole_numbers = lambda *shape: jax.ShapeDtypeStruct(shape, jnp.int32)
    pad = lambda halo: pltpu.VMEM((rows + 2 * halo, width), jnp.float32)
    work = lambda halo: pltpu.VMEM((fields, rows + 2 * halo, width), jnp.float32)
    params = pltpu.CompilerParams(vmem_limit_bytes=16 << 20)
    cells = fields * rows * width
    cost = pl.CostEstimate(flops=100 * cells, bytes_accessed=10 * cells, transcendentals=0)
    state_shape = floats(fields, rows, width)
    packed_shape = floats(2 * SLOTS + 2, rows // 2, width)
    edge_shape = floats(edge_planes(fields), REACH, width)
    in_vmem = pl.BlockSpec(memory_space=pltpu.VMEM)
    in_smem = pl.BlockSpec(memory_space=pltpu.SMEM)
    anywhere = pl.BlockSpec(memory_space=pl.ANY)

    upward, downward = pl.pallas_call(
        edge_kernel,
        in_specs=[anywhere] * 6,
        out_specs=(in_vmem, in_vmem),
        out_shape=(edge_shape, edge_shape),
        scratch_shapes=[pltpu.VMEM((2, REACH, width), jnp.int32), pltpu.SemaphoreType.DMA((20,))],
        compiler_params=params,
        cost_estimate=cost,
        name="edges",
    )(initial, adjoint, misfit, water_depth, drag_coef, wet_levels)
    above = shifted(downward, "tile", 1)
    below = shifted(upward, "tile", -1)

    wet, order, place, deepest = pl.pallas_call(
        plan_kernel,
        out_specs=(in_vmem,) * 3 + (in_smem,),
        out_shape=(floats(rows, width), whole_numbers(rows, width), whole_numbers(rows, width), whole_numbers(1, 1)),
        compiler_params=params,
        cost_estimate=cost,
        name="plan",
    )(wet_levels)

    pool = pl.BlockSpec((POOL, width), lambda i: (i, 0))
    raw = pl.pallas_call(
        pack_kernel,
        grid=(rows // POOL,),
        in_specs=[pl.BlockSpec((fields, POOL, width), lambda i: (0, i, 0)), pool, pool],
        out_specs=pl.BlockSpec((2 * SLOTS, POOL // 2, width), lambda i: (0, i, 0)),
        out_shape=floats(2 * SLOTS, rows // 2, width),
        compiler_params=params,
        cost_estimate=cost,
        name="pack",
    )(initial, wet, order)
    came_raw = passed_along(raw, "slab", 1)

    saved, surfaces = pl.pallas_call(
        forward_kernel,
        out_shape=(floats(SAVED, rows + 2 * HALO, width), floats(STEPS * rows + HALO, width)),
        scratch_shapes=[work(REACH)] + [pad(REACH)] * 13,
        compiler_params=params,
        cost_estimate=cost,
        name="forward",
    )(initial, above, below, water_depth, wet, drag_coef)
    came_surfaces = passed_along(surfaces, "slab", 1)

    start, gradient, start_packed = pl.pallas_call(
        adjoint_kernel,
        out_specs=(anywhere, in_vmem, in_vmem),
        out_shape=(state_shape, floats(rows, width), packed_shape),
        scratch_shapes=[work(0), pltpu.SemaphoreType.DMA(()), work(HALO)] + [pad(HALO)] * 14,
        compiler_params=params,
        cost_estimate=cost,
        name="adjoint",
    )(adjoint, misfit, saved, above, below, water_depth, wet, drag_coef, order)
    slabs = lax.axis_size("slab")
    if slabs > 4:
        gradients = [lax.psum(gradient, "slab")]
    else:
        gradients = [gradient] + [passed_along(gradient, "slab", distance) for distance in range(1, slabs)]
    start_packed, came_raw, came_surfaces = lax.optimization_barrier((start_packed, came_raw, came_surfaces))
    came_adjoint = passed_along(start_packed, "slab", -1)

    def unless_packed(sent, distance):
        return lax.cond(
            deepest[0, 0] > SLOTS,
            lambda sent: passed_along(sent, "slab", distance),
            lambda sent: pl.pallas_call(
                nothing_kernel, out_specs=anywhere, out_shape=state_shape, compiler_params=params, name="nothing"
            )(),
            sent,
        )

    next_state = pl.pallas_call(
        replay_kernel,
        in_specs=[in_smem] + [in_vmem] * 7 + [anywhere],
        out_shape=state_shape,
        scratch_shapes=[pad(0)] * 6,
        compiler_params=params,
        cost_estimate=cost,
        name="replay",
    )(deepest, came_raw, wet, order, place, water_depth, drag_coef, came_surfaces,
      unless_packed(initial, 1))

    pool = pl.BlockSpec((POOL, width), lambda i: (i, 0))
    next_adjoint, done = pl.pallas_call(
        unpack_kernel,
        grid=(rows // POOL,),
        in_specs=[in_smem, pl.BlockSpec((2 * SLOTS + 2, POOL // 2, width), lambda i: (0, i, 0)),
                  pool, pool, pool, anywhere],
        out_specs=[pl.BlockSpec((fields, POOL, width), lambda i: (0, i, 0)),
                   pl.BlockSpec((BLOCK, width), lambda i: (0, 0))],
        out_shape=[state_shape, floats(BLOCK, width)],
        compiler_params=params,
        cost_estimate=cost,
        name="unpack",
    )(deepest, came_adjoint, wet, order, place, unless_packed(start, -1))
    drag_total = pl.pallas_call(
        total_kernel, out_shape=floats(rows, width), compiler_params=params, cost_estimate=cost, name="total"
    )(done, *gradients)
    return (next_state[None], next_adjoint[None], drag_total)


def solution(mesh):
    return jax.shard_map(
        body,
        mesh=mesh,
        in_specs=(
            P(("groups", "slab"), None, "tile", None),
            P(("groups", "slab"), None, "tile", None),
            P(("groups", "slab"), None, "tile", None),
            P(("groups", "tile"), None),
            P(("groups", "tile"), None),
            P(("groups", "tile"), None),
            P(("groups", "tile"), None),
        ),
        out_specs=(
            P(("groups", "slab"), None, "tile", None),
            P(("groups", "slab"), None, "tile", None),
            P(("groups", "tile"), None),
        ),
        check_vma=False,
    )
```

```python
import jax
import jax.numpy as jnp
from jax import lax
from jax.experimental import pallas as pl
from jax.experimental.pallas import tpu as pltpu
from jax.sharding import PartitionSpec as P

STEPS = 4
BLOCK = 8
HALO = 2 * STEPS
REACH = 2 * HALO
SAVED = 2 + 2 * STEPS
POOL = 4 * BLOCK
SLOTS = 29
LEVELS = 24


def shifted(block, axis, distance):
    devices = range(lax.axis_size(axis))
    route = [(i - distance, i) for i in devices if i - distance in devices]
    return lax.ppermute(block, axis, route)


def passed_along(block, axis, distance):
    devices = range(lax.axis_size(axis))
    route = [((i - distance) % len(devices), i) for i in devices]
    return lax.ppermute(block, axis, route)


def row_diff(values):
    return pltpu.roll(values, values.shape[0] - 1, 0) - pltpu.roll(values, 1, 0)


def column_diff(values):
    width = values.shape[1]
    lane = lax.broadcasted_iota(jnp.int32, values.shape, 1)
    after = jnp.where(lane < width - 1, pltpu.roll(values, width - 1, 1), 0.0)
    before = jnp.where(lane > 0, pltpu.roll(values, 1, 1), 0.0)
    return after - before


def looped(count, visit):
    def one(index, carry):
        visit(pl.multiple_of(index * BLOCK, BLOCK))
        return carry

    lax.fori_loop(0, count // BLOCK, one, 0)


def over_blocks(rows, halo, visit, own, above, below):
    block = lambda start: pl.ds(start if isinstance(start, int) else pl.multiple_of(start, BLOCK), BLOCK)
    looped(halo, lambda start: visit(block(start), above, block(start)))
    looped(rows, lambda start: visit(block(start + halo), own, block(start)))
    looped(halo, lambda start: visit(block(start + halo + rows), below, block(start)))


def fill_padded(target, own, above, below):
    rows, halo = own.shape[0], above.shape[0]
    target[0:halo] = above
    target[halo : halo + rows] = own
    target[halo + rows : rows + 2 * halo] = below


class Shifted:
    def __init__(self, ref, at):
        self.ref, self.at = ref, at

    def __getitem__(self, key):
        return self.ref[key[0], self.at]


class AdjointEdge:
    def __init__(self, ref, fields):
        self.ref, self.fields = ref, fields

    def __getitem__(self, key):
        plane, rows = edge_place(self.fields, key[0])
        return self.ref[plane, rows]


def edge_planes(fields):
    return fields + 3 + (fields + STEPS + 1) // 2


def edge_place(fields, item):
    first = (fields + STEPS + 1) // 2
    half = 0 if item < first else HALO
    return fields + 3 + item - (first if half else 0), pl.ds(half, HALO)


def lanes_of(values):
    return lax.broadcasted_iota(jnp.int32, values.shape, values.ndim - 1)


def take_lanes(values, index):
    return jnp.take_along_axis(values, index, axis=1, mode="promise_in_bounds")


def plan_kernel(wet_levels, wet, order, place, deepest):
    rows, width = wet_levels.shape
    half = width // 2
    depth = wet_levels[...]
    wet[...] = depth.astype(jnp.float32)
    lane = lanes_of(depth)
    even = (lax.broadcasted_iota(jnp.int32, depth.shape, 0) // BLOCK) % 2 == 0
    most_levels = LEVELS
    before = lax.broadcasted_iota(jnp.int32, (width, 2 * width), 0) < lax.broadcasted_iota(jnp.int32, (width, 2 * width), 1)
    same = [jnp.where(depth == level, 1.0, 0.0) for level in range(most_levels, -1, -1)]
    counts = jnp.dot(
        jnp.concatenate(same).astype(jnp.bfloat16),
        jnp.where(before, 1.0, 0.0).astype(jnp.bfloat16),
        preferred_element_type=jnp.float32,
    )
    deeper = rank = jnp.zeros(depth.shape, jnp.float32)
    for index, level in enumerate(range(most_levels, -1, -1)):
        here = counts[index * rows : (index + 1) * rows]
        rank = jnp.where(depth == level, deeper + here[:, :width], rank)
        deeper = deeper + here[:, width:]
    rank = rank.astype(jnp.int32)
    ahead = jnp.where(rank < half, rank, width + half - 1 - rank)
    behind = jnp.where(rank < half, rank + half, width - 1 - rank)
    there = jnp.where(even, ahead, behind)
    place[...] = there
    moved = jnp.zeros_like(depth)
    for shift in range(1, width):
        moved = jnp.where(pltpu.roll(there, shift, 1) == lane, shift, moved)
    origin = (lane - moved) & (width - 1)
    order[...] = origin
    most = jnp.zeros((BLOCK, width), jnp.float32)
    for pool in range(rows // POOL):
        ats = [slice(pool * POOL + block * BLOCK, pool * POOL + (block + 1) * BLOCK) for block in range(4)]
        deep, shallow, swap = pair_up([take_lanes(wet[at], origin[at]) for at in ats])
        most = jnp.maximum(most, deep[0] + jnp.where(swap, shallow[1], shallow[0]))
        most = jnp.maximum(most, deep[1] + jnp.where(swap, shallow[0], shallow[1]))
    deepest[0, 0] = jnp.max(most).astype(jnp.int32)


def deep_and_shallow(blocks):
    first = lanes_of(blocks[0]) < blocks[0].shape[1] // 2
    deep = [jnp.where(first, blocks[0], blocks[1]), jnp.where(first, blocks[2], blocks[3])]
    shallow = [jnp.where(first, blocks[1], blocks[0]), jnp.where(first, blocks[3], blocks[2])]
    return deep, shallow


def pair_up(depths):
    deep, shallow = deep_and_shallow(depths)
    swap = (deep[0] - deep[1]) * (shallow[0] - shallow[1]) > 0.0
    return deep, shallow, swap


def pool_rows(pool):
    start = pl.multiple_of(pool * POOL, POOL)
    return [pl.ds(pl.multiple_of(start + block * BLOCK, BLOCK), BLOCK) for block in range(4)]


def pool_slots(pool):
    start = pl.multiple_of(pool * (POOL // 2), POOL // 2)
    return [pl.ds(pl.multiple_of(start + block * BLOCK, BLOCK), BLOCK) for block in range(2)]


def pack(state, wet, order, packed):
    levels = (state.shape[0] - 1) // 2

    def one_pool(pool, carry):
        ats = pool_rows(pool)
        slots = pool_slots(pool)
        orders = [order[at, :] for at in ats]
        deep_wet, _, swap = pair_up([take_lanes(wet[at, :], by) for at, by in zip(ats, orders)])
        for base, target in ((1, 0), (1 + levels, SLOTS)):

            def sorted_level(level):
                parts = [take_lanes(state[base + level, at, :], by) for at, by in zip(ats, orders)]
                deep, shallow = deep_and_shallow(parts)
                return deep, (jnp.where(swap, shallow[1], shallow[0]), jnp.where(swap, shallow[0], shallow[1]))

            for near in range((SLOTS + 1) // 2):
                far = SLOTS - 1 - near
                both = far < levels
                deep, shallow = sorted_level(near)
                far_deep, far_shallow = sorted_level(far) if both and far > near else (deep, shallow)
                for half in range(2):
                    value = deep[half]
                    if both:
                        value = jnp.where(deep_wet[half] > near, value, far_shallow[half])
                    packed[target + near, slots[half], :] = value
                    if far > near:
                        value = shallow[half]
                        if both:
                            value = jnp.where(deep_wet[half] > far, far_deep[half], value)
                        packed[target + far, slots[half], :] = value
        return carry

    lax.fori_loop(0, packed.shape[1] // (POOL // 2), one_pool, 0)


def pack_kernel(state, wet, order, packed):
    pack(state, wet, order, packed)


def unpack_pool(packed, wet, order, place, state, pool, state_pool):
    levels = (state.shape[0] - 1) // 2
    ats = pool_rows(pool)
    state_ats = pool_rows(state_pool)
    slots = pool_slots(pool)
    wets = [wet[at, :] for at in ats]
    places = [place[at, :] for at in ats]
    _, _, swap = pair_up([take_lanes(depth, order[at, :]) for depth, at in zip(wets, ats)])
    first = lanes_of(swap) < swap.shape[1] // 2
    for base, source in ((1, 0), (1 + levels, SLOTS)):

        def write_level(level, deep, ends):
            shallow = jnp.where(swap, ends[1], ends[0]), jnp.where(swap, ends[0], ends[1])
            for block in range(4):
                pair = deep[block // 2], shallow[block // 2]
                if block % 2:
                    pair = pair[::-1]
                value = take_lanes(jnp.where(first, *pair), places[block])
                state[base + level, state_ats[block], :] = jnp.where(wets[block] > level, value, 0.0)

        for near in range((SLOTS + 1) // 2):
            far = SLOTS - 1 - near
            head = [packed[source + near, slot, :] for slot in slots]
            tail = [packed[source + far, slot, :] for slot in slots]
            write_level(near, head, tail)
            if near < far < levels:
                write_level(far, tail, head)


def unpack_kernel(deepest, packed, wet, order, place, whole, state, done):
    done[...] = jnp.zeros_like(done)
    pool = pl.program_id(0)

    @pl.when(deepest[0, 0] > SLOTS)
    def _():
        pltpu.sync_copy(whole.at[:, pl.ds(pl.multiple_of(pool * POOL, POOL), POOL), :], state)

    @pl.when(deepest[0, 0] <= SLOTS)
    def _():
        unpack_pool(packed, wet, order, place, state, pool, 0)
        for half in range(2):
            at = pl.ds(pl.multiple_of(pool * (POOL // 2), POOL // 2), POOL // 2)
            state[0, half * (POOL // 2) : (half + 1) * (POOL // 2)] = packed[2 * SLOTS + half, at, :]


def replay_kernel(deepest, packed, wet, order, place, depth, drag, surfaces, whole, final,
                  thick, bot_u, bot_v, slope_x, slope_y, factor):
    fields, rows, width = final.shape
    levels = (fields - 1) // 2

    @pl.when(deepest[0, 0] > SLOTS)
    def _():
        pltpu.sync_copy(whole, final)
        for level in range(levels):
            active = wet[...] > level
            for at in (1 + level, 1 + levels + level):
                final[at] = jnp.where(active, final[at], 0.0)

    @pl.when(deepest[0, 0] <= SLOTS)
    def _():
        def one_pool(pool, carry):
            unpack_pool(packed, wet, order, place, final, pool, pool)
            return carry

        lax.fori_loop(0, rows // POOL, one_pool, 0)

    def lowest(start):
        at = pl.ds(start, BLOCK)
        wet_here = wet[at, :]
        low_u = low_v = jnp.zeros_like(wet_here)
        for level in range(levels):
            bottom = wet_here == level + 1
            low_u = jnp.where(bottom, final[1 + level, at, :], low_u)
            low_v = jnp.where(bottom, final[1 + levels + level, at, :], low_v)
        bot_u[at, :] = low_u
        bot_v[at, :] = low_v

    looped(rows, lowest)
    sea = jnp.minimum(wet[...], 1.0)
    thick[...] = depth[...] / jnp.maximum(wet[...], 1.0)
    for step in range(STEPS):
        surface = surfaces[step * rows : (step + 1) * rows]
        edges = surfaces[STEPS * rows : STEPS * rows + HALO]
        row = lax.broadcasted_iota(jnp.int32, surface.shape, 0)
        before = jnp.where(row == 0, edges[2 * step : 2 * step + 1], pltpu.roll(surface, 1, 0))
        after = jnp.where(row == rows - 1, edges[2 * step + 1 : 2 * step + 2], pltpu.roll(surface, rows - 1, 0))
        slope_x[...] = 0.2 * (after - before)
        slope_y[...] = 0.2 * column_diff(surface)
        factor[...] = drag_terms(bot_u[...], bot_v[...], thick[...], drag[...], sea)[2]

        def update(start):
            at = pl.ds(start, BLOCK)

            def store(level, u, v):
                final[1 + level, at, :] = u
                final[1 + levels + level, at, :] = v

            slow = factor[at, :]
            fetch = lambda level: (final[1 + level, at, :], final[1 + levels + level, at, :])
            _, low, _ = column_step(levels, wet[at, :], slow, slope_x[at, :], slope_y[at, :], fetch, store)
            bot_u[at, :] = slow * low[0]
            bot_v[at, :] = slow * low[1]

        looped(rows, update)
    final[0] = surfaces[(STEPS - 1) * rows : STEPS * rows]


def edge_kernel(state, adjoint, misfit, depth, drag, wet_levels, upward, downward, level_rows, sems):
    fields, rows, _ = state.shape
    first = (fields + STEPS + 1) // 2
    joint = fields + 3
    copies = []

    def bring(source, target):
        copies.append(pltpu.make_async_copy(source, target, sems.at[len(copies)]))

    for side, target in enumerate((upward, downward)):
        wide = pl.ds(side * (rows - REACH), REACH)
        narrow = pl.ds(side * (rows - HALO), HALO)
        bring(state.at[:, wide, :], target.at[pl.ds(0, fields)])
        bring(adjoint.at[pl.ds(0, first), narrow, :], target.at[pl.ds(joint, first), pl.ds(0, HALO), :])
        bring(
            adjoint.at[pl.ds(first, fields - first), narrow, :],
            target.at[pl.ds(joint, fields - first), pl.ds(HALO, HALO), :],
        )
        for step in range(STEPS):
            plane, at = edge_place(fields, fields + step)
            bring(misfit.at[step, narrow, :], target.at[plane, at, :])
        bring(depth.at[wide, :], target.at[fields])
        bring(drag.at[wide, :], target.at[fields + 2])
        bring(wet_levels.at[wide, :], level_rows.at[side])
    for copy in copies:
        copy.start()
    for copy in copies:
        copy.wait()
    for side, target in enumerate((upward, downward)):
        target[fields + 1] = level_rows[side].astype(jnp.float32)


def total_kernel(done, *refs):
    *gradients, total = refs
    summed = gradients[0][...]
    for gradient in gradients[1:]:
        summed = summed + gradient[...]
    total[...] = summed


def nothing_kernel(result):
    pass


def drag_terms(u_bottom, v_bottom, thickness, drag, sea):
    speed = jnp.sqrt(u_bottom * u_bottom + v_bottom * v_bottom + 0.0025)
    denominator = thickness + 0.1 * drag * speed + 1.0 - sea
    return speed, denominator, thickness / denominator


def column_step(levels, wet_here, slow, grad_x, grad_y, fetch, store):
    zero = jnp.zeros_like(wet_here)
    total = low = second = (zero, zero)
    u_up = v_up = zero
    u, v = fetch(0)
    for level in range(levels):
        u_down, v_down = fetch(level + 1) if level + 1 < levels else (zero, zero)
        inside = wet_here > level + 1
        bottom = wet_here == level + 1
        above_bottom = wet_here == level + 2
        own = 1.0 if level == 0 else 0.9
        weight = jnp.where(inside, own - 0.1, own)
        retain = jnp.where(inside, 1.0, jnp.where(bottom, slow, 0.0))
        ut = weight * u + 0.1 * (v + u_up + u_down) - grad_x
        vt = weight * v + 0.1 * (v_up + v_down - u) - grad_y
        low = jnp.where(bottom, ut, low[0]), jnp.where(bottom, vt, low[1])
        u_new = ut * retain
        v_new = vt * retain
        second = jnp.where(above_bottom, u_new, second[0]), jnp.where(above_bottom, v_new, second[1])
        store(level, u_new, v_new)
        total = total[0] + u_new, total[1] + v_new
        u_up, v_up, u, v = u, v, u_down, v_down
    return total, low, second


def forward_kernel(state, above, below, depth, wet, drag, saved, surfaces,
                   work, wet_pad, thick, drag_pad, eta, sum_u, sum_v, bot_u, bot_v, next_u, next_v,
                   slope_x, slope_y, factor):
    fields, rows, _ = state.shape
    levels = (fields - 1) // 2
    kept_rows = slice(HALO, REACH + HALO + rows)
    fill_padded(wet_pad, wet[...], above[fields + 1], below[fields + 1])
    fill_padded(drag_pad, drag[...], above[fields + 2], below[fields + 2])
    fill_padded(thick, depth[...], above[fields], below[fields])
    fill_padded(eta, state[0], above[0], below[0])
    thick[...] = thick[...] / jnp.maximum(wet_pad[...], 1.0)

    def sums(at, source, source_at):
        wet_here = wet_pad[at]
        total_u = total_v = low_u = low_v = jnp.zeros_like(wet_here)
        for level in range(levels):
            active = wet_here > level
            bottom = wet_here == level + 1
            u = jnp.where(active, source[1 + level, source_at], 0.0)
            v = jnp.where(active, source[1 + levels + level, source_at], 0.0)
            total_u += u
            total_v += v
            low_u = jnp.where(bottom, u, low_u)
            low_v = jnp.where(bottom, v, low_v)
        sum_u[at] = total_u
        sum_v[at] = total_v
        bot_u[at] = low_u
        bot_v[at] = low_v

    over_blocks(rows, REACH, sums, state, above, below)
    saved[0] = bot_u[kept_rows]
    saved[1] = bot_v[kept_rows]

    for step in range(STEPS):
        sea = jnp.minimum(wet_pad[...], 1.0)
        flux_x = thick[...] * sum_u[...]
        flux_y = thick[...] * sum_v[...]
        surface = sea * (eta[...] - 0.2 * (row_diff(flux_x) + column_diff(flux_y)))
        eta[...] = surface
        surfaces[step * rows : (step + 1) * rows] = eta[REACH : REACH + rows]
        surfaces[STEPS * rows + 2 * step : STEPS * rows + 2 * step + 1] = eta[REACH - 1 : REACH]
        surfaces[STEPS * rows + 2 * step + 1 : STEPS * rows + 2 * step + 2] = eta[REACH + rows : REACH + rows + 1]
        slope_x[...] = 0.2 * row_diff(surface)
        slope_y[...] = 0.2 * column_diff(surface)
        if step == STEPS - 1:
            weight = jnp.where(wet_pad[...] > 1.0, 0.9, 1.0)
            low_u, low_v = bot_u[...], bot_v[...]
            floor = wet_pad[...] > 0.0
            last_u = weight * low_u + 0.1 * (low_v + next_u[...]) - slope_x[...]
            last_v = weight * low_v + 0.1 * (next_v[...] - low_u) - slope_y[...]
            bot_u[...] = jnp.where(floor, last_u, 0.0)
            bot_v[...] = jnp.where(floor, last_v, 0.0)
        else:
            factor[...] = drag_terms(bot_u[...], bot_v[...], thick[...], drag_pad[...], sea)[2]

            def update(at, source, source_at):
                wet_here = wet_pad[at]

                def fetch(level):
                    u = source[1 + level, source_at]
                    v = source[1 + levels + level, source_at]
                    if step == 0:
                        u = jnp.where(wet_here > level, u, 0.0)
                        v = jnp.where(wet_here > level, v, 0.0)
                    return u, v

                def store(level, u, v):
                    work[1 + level, at] = u
                    work[1 + levels + level, at] = v

                total, low, second = column_step(
                    levels, wet_here, factor[at], slope_x[at], slope_y[at], fetch, store
                )
                sum_u[at], sum_v[at] = total
                bot_u[at], bot_v[at] = low
                next_u[at], next_v[at] = second

            if step == 0:
                over_blocks(rows, REACH, update, state, above, below)
            else:
                looped(rows + 2 * REACH, lambda start: update(pl.ds(start, BLOCK), work, pl.ds(start, BLOCK)))
        saved[2 + 2 * step] = bot_u[kept_rows]
        saved[3 + 2 * step] = bot_v[kept_rows]
        if step < STEPS - 1:
            bot_u[...] = factor[...] * bot_u[...]
            bot_v[...] = factor[...] * bot_v[...]


def adjoint_kernel(adjoint, misfit, kept, above, below, depth, wet, drag, order,
                   output, gradient, packed, start, sem,
                   work, wet_pad, thick, drag_pad, eta, sum_u, sum_v, bot_u, bot_v,
                   push_x, push_y, push_low_x, push_low_y, factor, grad_pad):
    fields, rows, _ = adjoint.shape
    levels = (fields - 1) // 2
    fill_padded(wet_pad, wet[...], above[fields + 1, HALO:], below[fields + 1, :HALO])
    fill_padded(drag_pad, drag[...], above[fields + 2, HALO:], below[fields + 2, :HALO])
    fill_padded(thick, depth[...], above[fields, HALO:], below[fields, :HALO])
    above = AdjointEdge(above, fields)
    below = AdjointEdge(below, fields)
    thick[...] = thick[...] / jnp.maximum(wet_pad[...], 1.0)
    fill_padded(eta, adjoint[0], above[0, :], below[0, :])
    grad_pad[...] = jnp.zeros_like(grad_pad)
    sea = jnp.minimum(wet_pad[...], 1.0)

    before = [(kept[0], kept[1])]
    for step in range(STEPS - 1):
        slow = drag_terms(*before[step], thick[...], drag_pad[...], sea)[2]
        before.append((slow * kept[2 + 2 * step], slow * kept[3 + 2 * step]))

    def sums(at, source, source_at):
        wet_here = wet_pad[at]
        total_u = total_v = low_u = low_v = jnp.zeros_like(wet_here)
        for level in range(levels):
            active = wet_here > level
            bottom = wet_here == level + 1
            u = jnp.where(active, source[1 + level, source_at], 0.0)
            v = jnp.where(active, source[1 + levels + level, source_at], 0.0)
            total_u += u
            total_v += v
            low_u = jnp.where(bottom, u, low_u)
            low_v = jnp.where(bottom, v, low_v)
        sum_u[at] = total_u
        sum_v[at] = total_v
        bot_u[at] = low_u
        bot_v[at] = low_v

    over_blocks(rows, HALO, sums, adjoint, above, below)

    for step in reversed(range(STEPS)):
        first, last = step == STEPS - 1, step == 0
        sea = jnp.minimum(wet_pad[...], 1.0)
        fill_padded(push_x, misfit[step], above[fields + step, :], below[fields + step, :])
        u_before, v_before = before[step]
        speed, denominator, slow = drag_terms(u_before, v_before, thick[...], drag_pad[...], sea)
        factor[...] = slow
        low_u, low_v = bot_u[...], bot_v[...]
        on_factor = low_u * kept[2 + 2 * step] + low_v * kept[3 + 2 * step]
        on_denominator = -on_factor * slow / denominator
        grad_pad[...] += 0.1 * speed * on_denominator
        on_speed = 0.1 * drag_pad[...] * on_denominator / speed
        loss = 1.0 - slow
        total_x = sum_u[...] - loss * low_u
        total_y = sum_v[...] - loss * low_v
        surface = sea * (eta[...] + push_x[...] + 0.2 * (row_diff(total_x) + column_diff(total_y)))
        eta[...] = surface
        thin = 0.2 * thick[...]
        toward_x = thin * row_diff(surface)
        toward_y = thin * column_diff(surface)
        push_x[...] = toward_x
        push_y[...] = toward_y
        push_low_x[...] = toward_x + on_speed * u_before
        push_low_y[...] = toward_y + on_speed * v_before

        def update(at, source, source_at, offset=0):
            if offset:
                at = source.at
            wet_here = wet_pad[at]
            slow_here = factor[at]
            along_x, along_y = push_x[at], push_y[at]
            low_x, low_y = push_low_x[at], push_low_y[at]
            zero = jnp.zeros_like(wet_here)
            total_u = total_v = low_u = low_v = zero

            def fetch(level):
                if level == levels:
                    return zero, zero
                retain = jnp.where(wet_here > level + 1, 1.0, jnp.where(wet_here > level, slow_here, 0.0))
                return retain * source[1 + level, source_at], retain * source[1 + levels + level, source_at]

            p_up = q_up = zero
            p, q = fetch(0)
            for level in range(levels):
                p_down, q_down = fetch(level + 1)
                inside = wet_here > level + 1
                bottom = wet_here == level + 1
                active = wet_here > level
                own = 1.0 if level == 0 else 0.9
                weight = jnp.where(inside, own - 0.1, own)
                u = weight * p + 0.1 * (p_up + p_down - q) + jnp.where(inside, along_x, low_x)
                v = weight * q + 0.1 * (q_up + q_down + p) + jnp.where(inside, along_y, low_y)
                u = jnp.where(active, u, 0.0)
                v = jnp.where(active, v, 0.0)
                if last:
                    start[1 + level, source_at] = u
                    start[1 + levels + level, source_at] = v
                else:
                    work[1 + level, at] = u
                    work[1 + levels + level, at] = v
                    total_u += u
                    total_v += v
                    low_u = jnp.where(bottom, u, low_u)
                    low_v = jnp.where(bottom, v, low_v)
                p_up, q_up, p, q = p, q, p_down, q_down
            if not last:
                sum_u[at] = total_u
                sum_v[at] = total_v
                bot_u[at] = low_u
                bot_v[at] = low_v

        if first:
            over_blocks(rows, HALO, update, adjoint, above, below)
        elif last:

            def into_start(begin):
                update(pl.ds(begin, BLOCK), Shifted(work, pl.ds(pl.multiple_of(begin + HALO, BLOCK), BLOCK)),
                       pl.ds(begin, BLOCK), HALO)

            looped(rows, into_start)
        else:

            def in_place(begin):
                at = pl.ds(begin, BLOCK)
                update(at, work, at)

            looped(rows + 2 * HALO, in_place)
    start[0] = eta[HALO : HALO + rows]
    gradient[...] = grad_pad[HALO : HALO + rows]
    copy = pltpu.make_async_copy(start, output, sem)
    copy.start()
    pack(start, wet, order, packed)
    for pool in range(rows // POOL):
        for half in range(2):
            at = pool * POOL + half * (POOL // 2)
            packed[2 * SLOTS + half, pool * (POOL // 2) : (pool + 1) * (POOL // 2)] = start[0, at : at + POOL // 2]
    copy.wait()


def body(start_states, end_adjoints, misfits, water_depth, drag_coef, sea_mask, bottom_level):
    initial = start_states[0]
    adjoint = end_adjoints[0]
    misfit = misfits[0]
    wet_levels = sea_mask * bottom_level
    fields, rows, width = initial.shape
    floats = lambda *shape: jax.ShapeDtypeStruct(shape, jnp.float32)
    whole_numbers = lambda *shape: jax.ShapeDtypeStruct(shape, jnp.int32)
    pad = lambda halo: pltpu.VMEM((rows + 2 * halo, width), jnp.float32)
    work = lambda halo: pltpu.VMEM((fields, rows + 2 * halo, width), jnp.float32)
    params = pltpu.CompilerParams(vmem_limit_bytes=16 << 20)
    cells = fields * rows * width
    cost = pl.CostEstimate(flops=100 * cells, bytes_accessed=10 * cells, transcendentals=0)
    state_shape = floats(fields, rows, width)
    packed_shape = floats(2 * SLOTS + 2, rows // 2, width)
    edge_shape = floats(edge_planes(fields), REACH, width)
    in_vmem = pl.BlockSpec(memory_space=pltpu.VMEM)
    in_smem = pl.BlockSpec(memory_space=pltpu.SMEM)
    anywhere = pl.BlockSpec(memory_space=pl.ANY)

    upward, downward = pl.pallas_call(
        edge_kernel,
        in_specs=[anywhere] * 6,
        out_specs=(in_vmem, in_vmem),
        out_shape=(edge_shape, edge_shape),
        scratch_shapes=[pltpu.VMEM((2, REACH, width), jnp.int32), pltpu.SemaphoreType.DMA((20,))],
        compiler_params=params,
        cost_estimate=cost,
        name="edges",
    )(initial, adjoint, misfit, water_depth, drag_coef, wet_levels)
    above = shifted(downward, "tile", 1)
    below = shifted(upward, "tile", -1)

    wet, order, place, deepest = pl.pallas_call(
        plan_kernel,
        out_specs=(in_vmem,) * 3 + (in_smem,),
        out_shape=(floats(rows, width), whole_numbers(rows, width), whole_numbers(rows, width), whole_numbers(1, 1)),
        compiler_params=params,
        cost_estimate=cost,
        name="plan",
    )(wet_levels)

    pool = pl.BlockSpec((POOL, width), lambda i: (i, 0))
    raw = pl.pallas_call(
        pack_kernel,
        grid=(rows // POOL,),
        in_specs=[pl.BlockSpec((fields, POOL, width), lambda i: (0, i, 0)), pool, pool],
        out_specs=pl.BlockSpec((2 * SLOTS, POOL // 2, width), lambda i: (0, i, 0)),
        out_shape=floats(2 * SLOTS, rows // 2, width),
        compiler_params=params,
        cost_estimate=cost,
        name="pack",
    )(initial, wet, order)
    came_raw = passed_along(raw, "slab", 1)

    saved, surfaces = pl.pallas_call(
        forward_kernel,
        out_shape=(floats(SAVED, rows + 2 * HALO, width), floats(STEPS * rows + HALO, width)),
        scratch_shapes=[work(REACH)] + [pad(REACH)] * 13,
        compiler_params=params,
        cost_estimate=cost,
        name="forward",
    )(initial, above, below, water_depth, wet, drag_coef)
    came_surfaces = passed_along(surfaces, "slab", 1)

    start, gradient, start_packed = pl.pallas_call(
        adjoint_kernel,
        out_specs=(anywhere, in_vmem, in_vmem),
        out_shape=(state_shape, floats(rows, width), packed_shape),
        scratch_shapes=[work(0), pltpu.SemaphoreType.DMA(()), work(HALO)] + [pad(HALO)] * 14,
        compiler_params=params,
        cost_estimate=cost,
        name="adjoint",
    )(adjoint, misfit, saved, above, below, water_depth, wet, drag_coef, order)
    slabs = lax.axis_size("slab")
    if slabs > 4:
        gradients = [lax.psum(gradient, "slab")]
    else:
        gradients = [gradient] + [passed_along(gradient, "slab", distance) for distance in range(1, slabs)]
    start_packed, came_raw, came_surfaces = lax.optimization_barrier((start_packed, came_raw, came_surfaces))
    came_adjoint = passed_along(start_packed, "slab", -1)

    def unless_packed(sent, distance):
        return lax.cond(
            deepest[0, 0] > SLOTS,
            lambda sent: passed_along(sent, "slab", distance),
            lambda sent: pl.pallas_call(
                nothing_kernel, out_specs=anywhere, out_shape=state_shape, compiler_params=params, name="nothing"
            )(),
            sent,
        )

    next_state = pl.pallas_call(
        replay_kernel,
        in_specs=[in_smem] + [in_vmem] * 7 + [anywhere],
        out_shape=state_shape,
        scratch_shapes=[pad(0)] * 6,
        compiler_params=params,
        cost_estimate=cost,
        name="replay",
    )(deepest, came_raw, wet, order, place, water_depth, drag_coef, came_surfaces,
      unless_packed(initial, 1))

    pool = pl.BlockSpec((POOL, width), lambda i: (i, 0))
    next_adjoint, done = pl.pallas_call(
        unpack_kernel,
        grid=(rows // POOL,),
        in_specs=[in_smem] + [in_vmem] * 4 + [anywhere],
        out_specs=[pl.BlockSpec((fields, POOL, width), lambda i: (0, i, 0)),
                   pl.BlockSpec((BLOCK, width), lambda i: (0, 0))],
        out_shape=[state_shape, floats(BLOCK, width)],
        compiler_params=params,
        cost_estimate=cost,
        name="unpack",
    )(deepest, came_adjoint, wet, order, place, unless_packed(start, -1))
    drag_total = pl.pallas_call(
        total_kernel, out_shape=floats(rows, width), compiler_params=params, cost_estimate=cost, name="total"
    )(done, *gradients)
    return (next_state[None], next_adjoint[None], drag_total)


def solution(mesh):
    return jax.shard_map(
        body,
        mesh=mesh,
        in_specs=(
            P(("groups", "slab"), None, "tile", None),
            P(("groups", "slab"), None, "tile", None),
            P(("groups", "slab"), None, "tile", None),
            P(("groups", "tile"), None),
            P(("groups", "tile"), None),
            P(("groups", "tile"), None),
            P(("groups", "tile"), None),
        ),
        out_specs=(
            P(("groups", "slab"), None, "tile", None),
            P(("groups", "slab"), None, "tile", None),
            P(("groups", "tile"), None),
        ),
        check_vma=False,
    )
```
